32 devices in a mesh: shot: 8 (over z, y), rcv: 4 (over x, core).
Axes of the slice: x: 2, y: 2, z: 4, core: 2. Of those that a mesh axis runs over, the one named last changes fastest.
Arguments:
- data_matrix: bfloat16 [2, 16, 1024, 1024], P(None, None, 'shot', 'rcv'), may hold values from -12 to 12
- shot_records: bfloat16 [2, 16, 1024, 1024], P(None, None, 'rcv', 'shot'), may hold values from -4 to 4
- live: int32 [1024, 1024], P('rcv', 'shot'), may hold values 0 or 1
Outputs:
- predicted: bfloat16 [2, 16, 1024, 1024], P(None, None, 'rcv', 'shot')
- primaries: bfloat16 [2, 16, 1024, 1024], P(None, None, 'rcv', 'shot')
The draws below stay inside these ranges and needn't reach their ends.
All inputs are finite; a program needn't handle non-finite values. No bound on the sum of `live` on one device may be relied on, other than what follows from the above.
Results may differ from the reference program's by a relative error of at most 0.013.
Values may be sent and summed in bfloat16 or wider, within the bound.
A program may use at most 128 MiB of HBM per device.

```python
import math
import jax
import jax.numpy as jnp
from jax import lax

NPTS = 1024
F_WIN = 16
SHOTS = 1024
N_RCV = 4


def draw_data_matrix(key, part):
    first, second, third = jax.random.split(key, 3)
    shape = (2, F_WIN, NPTS, NPTS)
    noise = jnp.clip(jax.random.normal(first, shape, jnp.float32), -4.0, 4.0)
    place = jnp.arange(NPTS, dtype=jnp.float32) / (NPTS - 1)
    rough = jax.random.uniform(second, (NPTS,), jnp.float32, -0.5, 0.5)
    scale = jnp.exp(math.log(3.0) * place + math.log(10.0) * rough)
    gain = jax.random.uniform(third, (2, F_WIN, NPTS), jnp.float32, 0.5, 1.0)
    rows = jnp.arange(NPTS)
    eye = (rows[:, None] == rows[None, :]).astype(jnp.float32)
    values = (gain[..., None] * eye + 0.5 * noise / math.sqrt(NPTS)) * scale[:, None]
    return values.astype(jnp.bfloat16)


def draw_shot_records(key, part):
    first, second = jax.random.split(key, 2)
    shape = (2, F_WIN, NPTS, SHOTS)
    noise = jnp.clip(jax.random.normal(first, shape, jnp.float32), -4.0, 4.0)
    scale = 0.1 * jnp.exp(math.log(10.0) * jax.random.uniform(second, (SHOTS,), jnp.float32, 0.0, 1.0))
    return (noise * scale).astype(jnp.bfloat16)


def place_ends(values, rng, smallest, top_value):
    spot = [jax.random.randint(jax.random.fold_in(rng, axis), (), 0, length) for axis, length in enumerate(values.shape)]
    main_axis = values.shape.index(max(values.shape))
    next_to = spot[:main_axis] + [(spot[main_axis] + 1) % values.shape[main_axis]] + spot[main_axis + 1:]
    return values.at[tuple(spot)].set(smallest).at[tuple(next_to)].set(top_value)


def setup_inputs(seed: int = 0) -> dict:
    streams_of = jax.random.split(jax.random.key(seed), 4)
    return {
        "data_matrix": draw_data_matrix(jax.random.fold_in(streams_of[3], 71), 0),
        "shot_records": draw_shot_records(jax.random.fold_in(streams_of[3], 71), 0),
        "live": place_ends((jax.random.randint(streams_of[2], (NPTS, SHOTS), 0, 8) < 7).astype(jnp.int32), jax.random.fold_in(streams_of[2], 1), 0, 1),
    }


def one_slice(inputs):
    matrix, records = inputs
    group = NPTS // N_RCV
    total = jnp.zeros((2, NPTS, records.shape[2]), jnp.float32)
    for index in range(N_RCV):
        left = matrix[:, :, index * group:(index + 1) * group].astype(jnp.float32)
        right = records[:, index * group:(index + 1) * group, :].astype(jnp.float32)
        prod = jnp.einsum("ark,bks->abrs", left, right)
        term = jnp.stack((prod[0, 0] - prod[1, 1], prod[0, 1] + prod[1, 0])).astype(jnp.bfloat16)
        term = lax.optimization_barrier(term)
        total = total + term.astype(jnp.float32)
    return total


def reference(data_matrix, shot_records, live):
    records = shot_records * live.astype(jnp.bfloat16)[None, None]
    slices = lax.map(one_slice, (jnp.moveaxis(data_matrix, 1, 0), jnp.moveaxis(records, 1, 0)))
    total = jnp.moveaxis(slices, 0, 1)
    rec = records.astype(jnp.float32)
    num_re = jnp.mean(total[0] * rec[0] + total[1] * rec[1], axis=1)
    num_im = jnp.mean(total[0] * rec[1] - total[1] * rec[0], axis=1)
    power = jnp.mean(total[0] * total[0] + total[1] * total[1], axis=1) + 1e-6
    filt_re = (num_re / power)[:, None, :]
    filt_im = (num_im / power)[:, None, :]
    out_re = rec[0] - (filt_re * total[0] - filt_im * total[1])
    out_im = rec[1] - (filt_re * total[1] + filt_im * total[0])
    primaries = jnp.stack((out_re, out_im)).astype(jnp.bfloat16)
    return total.astype(jnp.bfloat16), primaries
```

```python
import functools

import jax
import jax.numpy as jnp
from jax import lax
from jax.experimental import pallas as pl
from jax.experimental.pallas import tpu as pltpu
from jax.sharding import PartitionSpec as P

MESH = pl.DeviceIdType.MESH


def each(start, stop, body):
    def step(index, carry):
        body(index)
        return carry

    lax.fori_loop(start, stop, step, 0)


def exchange_kernel(
    n_shot, n_rcv, side,
    d_ref, s_ref, live_ref, o_ref, filt_ref,
    dbuf, pbuf, srec, live_v, rec, mbuf, fbuf, acc,
    load_sem, d_send, d_recv, dl_send, p_send, p_recv, pl_send, o_send, o_recv, f_send, f_recv,
):
    n_freq, own_rows = d_ref.shape[1], d_ref.shape[2]
    own_pts, own_shots = s_ref.shape[2], s_ref.shape[3]
    points = own_pts * n_rcv
    plane = side * n_rcv
    slots = n_freq // plane
    near = 2 * side
    n_groups = n_shot // near
    per_rcv = own_pts // own_rows
    me_i, me_j = lax.axis_index("shot"), lax.axis_index("rcv")
    group, b_me = lax.div(me_i, near), lax.rem(me_i, near)
    half, y = lax.div(b_me, side), lax.rem(me_i, side)
    place = y * n_rcv + me_j

    def owner_half(g):
        return jnp.where(g < n_groups // 2, 1, 0)

    mine = owner_half(group)
    owner = half == mine
    relay = jnp.logical_not(owner)
    own_base = group * near + mine * side
    far_base = group * near + (1 - mine) * side
    plane_base = group * near + half * side
    has_left = jnp.logical_and(owner, group > 0)
    has_right = jnp.logical_and(owner, group < n_groups - 1)
    left = ((group - 1) * near + owner_half(group - 1) * side + y, me_j)
    right = ((group + 1) * near + owner_half(group + 1) * side + y, me_j)
    head = (own_base + y, me_j)

    load_s = pltpu.make_async_copy(s_ref, srec, load_sem.at[0])
    load_live = pltpu.make_async_copy(live_ref, live_v, load_sem.at[1])
    load_s.start()
    load_live.start()

    barrier = pltpu.get_barrier_semaphore()
    n_near = near * n_rcv

    def greet(k):
        other = lax.rem(b_me * n_rcv + me_j + k, n_near)
        target = (group * near + lax.div(other, n_rcv), lax.rem(other, n_rcv))
        pl.semaphore_signal(barrier, inc=1, device_id=target, device_id_type=MESH)

    each(1, n_near, greet)
    for there, target in ((has_left, left), (has_right, right)):
        @pl.when(there)
        def _():
            pl.semaphore_signal(barrier, inc=1, device_id=target, device_id_type=MESH)

    load_s.wait()
    load_live.wait()

    def mask(f):
        keep = live_v[...].astype(jnp.bfloat16)
        rec[f, :, :own_shots] = srec[0, f] * keep
        rec[f, :, own_shots:] = srec[1, f] * keep

    each(0, n_freq, mask)
    acc[...] = jnp.zeros_like(acc)
    pl.semaphore_wait(barrier, n_near - 1 + has_left.astype(jnp.int32) + has_right.astype(jnp.int32))

    def rows_of(i, size):
        return pl.ds(pl.multiple_of(i * size, size), size)

    def remote(src, dst, target, send_sem, recv_sem):
        pltpu.make_async_remote_copy(
            src_ref=src, dst_ref=dst, send_sem=send_sem, recv_sem=recv_sem,
            device_id=target, device_id_type=MESH,
        ).start()

    def send(src, dst, target, send_sem, recv_sem):
        here = jnp.logical_and(target[0] == me_i, target[1] == me_j)

        @pl.when(here)
        def _():
            pltpu.make_async_copy(src, dst, recv_sem).start()

        @pl.when(jnp.logical_not(here))
        def _():
            remote(src, dst, target, send_sem, recv_sem)

    def sent(src, target, send_sem):
        here = jnp.logical_and(target[0] == me_i, target[1] == me_j)

        @pl.when(jnp.logical_not(here))
        def _():
            done(src, send_sem)

    def done(ref, sem):
        pltpu.make_async_copy(ref, ref, sem).wait()

    def partner(t):
        dy, dx, dc = lax.div(t, n_rcv), lax.div(lax.rem(t, n_rcv), 2), lax.rem(t, 2)
        py = lax.rem(y + dy, side)
        px = lax.rem(lax.div(me_j, 2) + dx, n_rcv // 2)
        pj = px * 2 + lax.rem(me_j + dc, 2)
        return py, pj

    def source(t):
        dy, dx, dc = lax.div(t, n_rcv), lax.div(lax.rem(t, n_rcv), 2), lax.rem(t, 2)
        py = lax.rem(y + side - dy, side)
        px = lax.rem(lax.div(me_j, 2) + n_rcv // 2 - dx, n_rcv // 2)
        pj = px * 2 + lax.rem(me_j + dc, 2)
        return py, pj

    def freq(s, py, pj):
        return s * plane + py * n_rcv + pj

    def d_block(s, i, j):
        return dbuf.at[s, j, :, rows_of(i, own_rows), :]

    def p_block(s, b, j):
        return pbuf.at[s, b, rows_of(j, own_pts), :]

    def send_d(s, t):
        py, pj = partner(t)
        remote(
            d_ref.at[:, freq(s, py, pj)], d_block(s, me_i, me_j), (plane_base + py, pj),
            d_send.at[s, t], d_recv.at[s, me_i, me_j],
        )

    def send_p(s, t):
        py, pj = partner(t)
        remote(
            rec.at[freq(s, py, pj)], p_block(s, b_me, me_j), (plane_base + py, pj),
            p_send.at[s, t], p_recv.at[s, b_me, me_j],
        )

    def pass_on(src, s, i, j, to_left, to_right):
        for way, there, target in ((0, to_left, left), (1, to_right, right)):
            @pl.when(there)
            def _():
                remote(src, d_block(s, i, j), target, dl_send.at[way, s, i], d_recv.at[s, i, j])

    def my_f(s):
        return freq(s, y, me_j)

    def for_slots(start, stop, body):
        each(0, slots, lambda s: each(start, stop, lambda t: body(s, t)))

    def p_up(s, t):
        py, pj = source(t)
        b = half * side + py
        done(p_block(s, b, pj), p_recv.at[s, b, pj])
        remote(p_block(s, b, pj), p_block(s, b, pj), head, pl_send.at[s, b], p_recv.at[s, b, pj])

    def d_up(s, t):
        py, pj = source(t)
        i = far_base + py
        done(d_block(s, i, pj), d_recv.at[s, i, pj])
        remote(d_block(s, i, pj), d_block(s, i, pj), head, dl_send.at[0, s, i], d_recv.at[s, i, pj])

    @pl.when(relay)
    def _():
        def own_p(s):
            remote(
                rec.at[my_f(s)], p_block(s, b_me, me_j), head, pl_send.at[s, b_me], p_recv.at[s, b_me, me_j]
            )

        def own_d(s):
            remote(
                d_ref.at[:, my_f(s)], d_block(s, me_i, me_j), head,
                dl_send.at[0, s, me_i], d_recv.at[s, me_i, me_j],
            )

        each(0, slots, own_p)
        for_slots(1, plane, send_p)
        for_slots(1, plane, send_d)
        for_slots(1, plane, p_up)

        def rest(s):
            own_d(s)
            each(1, plane, lambda t: d_up(s, t))

        each(0, slots, rest)

    def take_rows(s, i, to_left, to_right):
        def one(j):
            done(d_block(s, i, j), d_recv.at[s, i, j])
            pass_on(d_block(s, i, j), s, i, j, to_left, to_right)

        each(0, n_rcv, one)

    def take_far(s, k):
        i = far_base + lax.rem(y + side - k, side)

        def one(t):
            pj = source(t)[1]
            done(d_block(s, i, pj), d_recv.at[s, i, pj])
            pass_on(d_block(s, i, pj), s, i, pj, has_left, has_right)

        each(0, n_rcv, one)
        return i

    def take_other(s, hh, near_plane, k):
        other = lax.rem(group + hh, n_groups)
        nearer = owner_half(other)
        i = other * near + (nearer if near_plane else 1 - nearer) * side + lax.rem(y + side - k, side)
        from_left = other < group
        if n_groups > 2:
            take_rows(
                s, i, jnp.logical_and(has_left, jnp.logical_not(from_left)), jnp.logical_and(has_right, from_left)
            )
        else:
            each(0, n_rcv, lambda j: done(d_block(s, i, j), d_recv.at[s, i, j]))
        return i

    def compute(s, i):
        rows = rows_of(i, own_rows)
        j = lax.div(i, per_rcv)

        def one(n):
            b = lax.rem(n + b_me, near)
            total = None
            for h in range(n_rcv):
                block = pbuf[s, b, h * own_pts:(h + 1) * own_pts, :]
                lhs = dbuf[s, h, :, rows, :].reshape(2 * own_rows, own_pts)
                prod = jnp.dot(lhs, block, preferred_element_type=jnp.float32)
                total = prod if total is None else total + prod
            m_re = total[:own_rows, :own_shots] - total[own_rows:, own_shots:]
            m_im = total[:own_rows, own_shots:] + total[own_rows:, :own_shots]
            mbuf[s, b, rows, :own_shots] = m_re.astype(jnp.bfloat16)
            mbuf[s, b, rows, own_shots:] = m_im.astype(jnp.bfloat16)
            dst = o_ref.at[my_f(s), rows_of(lax.rem(i, per_rcv), own_rows), :]
            send(mbuf.at[s, b, rows, :], dst, (group * near + b, j), o_send.at[s, b, j], o_recv.at[my_f(s)])
            p_re = pbuf[s, b, rows, :own_shots].astype(jnp.float32)
            p_im = pbuf[s, b, rows, own_shots:].astype(jnp.float32)

            def down(value):
                return jnp.sum(value.reshape(own_rows // 8, 8, own_shots), axis=0)

            acc[s, b, 0] += down(m_re * p_re + m_im * p_im)
            acc[s, b, 1] += down(m_re * p_im - m_im * p_re)
            acc[s, b, 2] += down(m_re * m_re + m_im * m_im)

        each(0, near, one)

    def coefficients(s):
        def one(n):
            b = lax.rem(n + b_me, near)
            num_re, num_im, power = (
                jnp.sum(acc[s, b, v], axis=0, keepdims=True) / float(points) for v in range(3)
            )
            power = power + 1e-6
            row = lax.broadcasted_iota(jnp.int32, (8, own_shots), 0)
            fbuf[s, b] = jnp.where(row < 4, num_re / power, num_im / power)
            for j in range(n_rcv):
                send(
                    fbuf.at[s, b], filt_ref.at[my_f(s)], (group * near + b, j),
                    f_send.at[s, b, j], f_recv.at[my_f(s)],
                )

        each(0, near, one)

    @pl.when(owner)
    def _():
        def own_d(s):
            src = d_ref.at[:, my_f(s)]
            pass_on(src, s, me_i, me_j, has_left, has_right)
            pltpu.make_async_copy(src, d_block(s, me_i, me_j), d_recv.at[s, me_i, me_j]).start()
            pltpu.make_async_copy(
                rec.at[my_f(s)], p_block(s, b_me, me_j), p_recv.at[s, b_me, me_j]
            ).start()

        each(0, slots, own_d)
        for_slots(1, plane, send_d)
        for_slots(1, plane, send_p)

        def in_plane(s, t):
            py, pj = source(t)
            i = own_base + py
            done(d_block(s, i, pj), d_recv.at[s, i, pj])
            pass_on(d_block(s, i, pj), s, i, pj, has_left, has_right)

        for_slots(1, plane, in_plane)

        def first(s):
            done(d_block(s, me_i, me_j), d_recv.at[s, me_i, me_j])
            each(0, n_near, lambda n: done(
                p_block(s, lax.div(n, n_rcv), lax.rem(n, n_rcv)), p_recv.at[s, lax.div(n, n_rcv), lax.rem(n, n_rcv)]
            ))
            each(0, side, lambda k: compute(s, own_base + k))
            each(1, n_groups, lambda hh: each(0, side, lambda k: compute(s, take_other(s, hh, True, k))))

        each(0, slots, first)

        def others(u):
            s, k = lax.div(u, side), lax.rem(u, side)
            each(1, n_groups, lambda hh: compute(s, take_other(s, hh, False, k)))
            pl.when(k == side - 1)(lambda: coefficients(s))

        def second(u):
            s, k = lax.div(u, side), lax.rem(u, side)
            compute(s, take_far(s, k))
            pl.when(u > 0)(lambda: others(u - 1))

        each(0, slots * side, second)
        others(slots * side - 1)

    def result_arrived(n):
        done(o_ref.at[n], o_recv.at[n])
        done(filt_ref.at[n], f_recv.at[n])

    each(0, n_freq, result_arrived)
    for_slots(1, plane, lambda s, t: done(d_ref.at[:, 0], d_send.at[s, t]))
    for_slots(1, plane, lambda s, t: done(rec.at[0], p_send.at[s, t]))

    def rows_sent(way, s, i):
        done(dbuf.at[s, :, :, rows_of(i, own_rows), :], dl_send.at[way, s, i])

    @pl.when(relay)
    def _():
        def one(s, k):
            rows_sent(0, s, far_base + k)
            done(pbuf.at[s, half * side + k], pl_send.at[s, half * side + k])

        for_slots(0, side, one)

    @pl.when(owner)
    def _():
        first_row, end_row = group * near, group * near + near
        pl.when(has_left)(lambda: for_slots(first_row, n_shot, lambda s, i: rows_sent(0, s, i)))
        pl.when(has_right)(lambda: for_slots(0, end_row, lambda s, i: rows_sent(1, s, i)))

        def results(s, n):
            b, j = lax.div(n, n_rcv), lax.rem(n, n_rcv)
            target = (group * near + b, j)
            sent(fbuf.at[s, b], target, f_send.at[s, b, j])
            sent(mbuf.at[s, b, rows_of(j, own_pts), :], target, o_send.at[s, b, j])

        for_slots(0, n_near, results)


def subtract_kernel(o_ref, filt_ref, s_ref, live_ref, pred_ref, prim_ref):
    shots = s_ref.shape[3]
    keep = live_ref[...].astype(jnp.bfloat16)
    for f in range(o_ref.shape[0]):
        re, im = o_ref[f, :, :shots], o_ref[f, :, shots:]
        pred_ref[0, f] = re
        pred_ref[1, f] = im
        re, im = re.astype(jnp.float32), im.astype(jnp.float32)
        filt_re, filt_im = filt_ref[f, 0:1, :], filt_ref[f, 4:5, :]
        rec_re = (s_ref[0, f] * keep).astype(jnp.float32)
        rec_im = (s_ref[1, f] * keep).astype(jnp.float32)
        prim_ref[0, f] = (rec_re - (filt_re * re - filt_im * im)).astype(jnp.bfloat16)
        prim_ref[1, f] = (rec_im - (filt_re * im + filt_im * re)).astype(jnp.bfloat16)


def shards(n_shot, n_rcv, data_matrix, shot_records, live):
    _, n_freq, own_rows, own_pts = data_matrix.shape
    own_shots = shot_records.shape[3]
    points = own_pts * n_rcv
    side = 2
    slots, near = n_freq // (side * n_rcv), 2 * side
    anywhere = pl.BlockSpec(memory_space=pl.ANY)
    dma = pltpu.SemaphoreType.DMA
    multiples, filt = pl.pallas_call(
        functools.partial(exchange_kernel, n_shot, n_rcv, side),
        out_shape=(
            jax.ShapeDtypeStruct((n_freq, own_pts, 2 * own_shots), jnp.bfloat16),
            jax.ShapeDtypeStruct((n_freq, 8, own_shots), jnp.float32),
        ),
        in_specs=[anywhere] * 3,
        out_specs=(anywhere, anywhere),
        scratch_shapes=[
            pltpu.VMEM((slots, n_rcv, 2, points, own_pts), jnp.bfloat16),
            pltpu.VMEM((slots, near, points, 2 * own_shots), jnp.bfloat16),
            pltpu.VMEM((2, n_freq, own_pts, own_shots), jnp.bfloat16),
            pltpu.VMEM((own_pts, own_shots), jnp.int32),
            pltpu.VMEM((n_freq, own_pts, 2 * own_shots), jnp.bfloat16),
            pltpu.VMEM((slots, near, points, 2 * own_shots), jnp.bfloat16),
            pltpu.VMEM((slots, near, 8, own_shots), jnp.float32),
            pltpu.VMEM((slots, near, 3, 8, own_shots), jnp.float32),
            dma((2,)),
            dma((slots, side * n_rcv)),
            dma((slots, n_shot, n_rcv)),
            dma((2, slots, n_shot)),
            dma((slots, side * n_rcv)),
            dma((slots, near, n_rcv)),
            dma((slots, near)),
            dma((slots, near, n_rcv)),
            dma((n_freq,)),
            dma((slots, near, n_rcv)),
            dma((n_freq,)),
        ],
        compiler_params=pltpu.CompilerParams(
            collective_id=0, has_side_effects=True, vmem_limit_bytes=60 * 1024 * 1024
        ),
    )(data_matrix, shot_records, live)
    step = 4
    pair = pl.BlockSpec((2, step, own_pts, own_shots), lambda f: (0, f, 0, 0))
    out = jax.ShapeDtypeStruct((2, n_freq, own_pts, own_shots), jnp.bfloat16)
    return pl.pallas_call(
        subtract_kernel,
        grid=(n_freq // step,),
        out_shape=(out, out),
        in_specs=[
            pl.BlockSpec((step, own_pts, 2 * own_shots), lambda f: (f, 0, 0)),
            pl.BlockSpec((step, 8, own_shots), lambda f: (f, 0, 0)),
            pair,
            pl.BlockSpec((own_pts, own_shots), lambda f: (0, 0)),
        ],
        out_specs=(pair, pair),
        compiler_params=pltpu.CompilerParams(vmem_limit_bytes=24 * 1024 * 1024),
    )(multiples, filt, shot_records, live)


def solution(mesh):
    in_specs = (P(None, None, "shot", "rcv"), P(None, None, "rcv", "shot"), P("rcv", "shot"))
    out_specs = (P(None, None, "rcv", "shot"), P(None, None, "rcv", "shot"))
    body = functools.partial(shards, mesh.shape["shot"], mesh.shape["rcv"])
    return jax.shard_map(body, mesh=mesh, in_specs=in_specs, out_specs=out_specs, check_vma=False)
```

```python
import functools

import jax
import jax.numpy as jnp
from jax import lax
from jax.experimental import pallas as pl
from jax.experimental.pallas import tpu as pltpu
from jax.sharding import PartitionSpec as P

MESH = pl.DeviceIdType.MESH


def each(start, stop, body):
    def step(index, carry):
        body(index)
        return carry

    lax.fori_loop(start, stop, step, 0)


def exchange_kernel(
    n_shot, n_rcv, side, cuts,
    d_ref, s_ref, live_ref, o_ref, filt_ref, rec,
    dbuf, pbuf, srec, live_v, mbuf, fbuf, acc,
    load_sem, d_send, d_recv, dl_send, p_send, p_recv, pl_send, o_send, o_recv, f_send, f_recv,
):
    n_freq, own_rows = d_ref.shape[1], d_ref.shape[2]
    own_pts, own_shots = s_ref.shape[2], s_ref.shape[3]
    points = own_pts * n_rcv
    plane = side * n_rcv
    slots = n_freq // plane
    near = 2 * side
    n_groups = n_shot // near
    unit = own_rows // cuts
    me_i, me_j = lax.axis_index("shot"), lax.axis_index("rcv")
    group, b_me = lax.div(me_i, near), lax.rem(me_i, near)
    half, y = lax.div(b_me, side), lax.rem(me_i, side)
    place = y * n_rcv + me_j

    def owner_half(g):
        return jnp.where(g < n_groups // 2, 1, 0)

    mine = owner_half(group)
    owner = half == mine
    relay = jnp.logical_not(owner)
    own_base = group * near + mine * side
    far_base = group * near + (1 - mine) * side
    plane_base = group * near + half * side
    has_left = jnp.logical_and(owner, group > 0)
    has_right = jnp.logical_and(owner, group < n_groups - 1)
    left = ((group - 1) * near + owner_half(group - 1) * side + y, me_j)
    right = ((group + 1) * near + owner_half(group + 1) * side + y, me_j)
    head = (own_base + y, me_j)

    load_s = pltpu.make_async_copy(s_ref, srec, load_sem.at[0])
    load_live = pltpu.make_async_copy(live_ref, live_v, load_sem.at[1])
    load_s.start()
    load_live.start()

    barrier = pltpu.get_barrier_semaphore()
    n_near = near * n_rcv

    def greet(k):
        other = lax.rem(b_me * n_rcv + me_j + k, n_near)
        target = (group * near + lax.div(other, n_rcv), lax.rem(other, n_rcv))
        pl.semaphore_signal(barrier, inc=1, device_id=target, device_id_type=MESH)

    each(1, n_near, greet)
    for there, target in ((has_left, left), (has_right, right)):
        @pl.when(there)
        def _():
            pl.semaphore_signal(barrier, inc=1, device_id=target, device_id_type=MESH)

    load_s.wait()
    load_live.wait()

    def mask(f):
        keep = live_v[...].astype(jnp.bfloat16)
        rec[f, :, :own_shots] = srec[0, f] * keep
        rec[f, :, own_shots:] = srec[1, f] * keep

    each(0, n_freq, mask)
    acc[...] = jnp.zeros_like(acc)
    pl.semaphore_wait(barrier, n_near - 1 + has_left.astype(jnp.int32) + has_right.astype(jnp.int32))

    def rows_of(i, size):
        return pl.ds(pl.multiple_of(i * size, size), size)

    def remote(src, dst, target, send_sem, recv_sem):
        pltpu.make_async_remote_copy(
            src_ref=src, dst_ref=dst, send_sem=send_sem, recv_sem=recv_sem,
            device_id=target, device_id_type=MESH,
        ).start()

    def send(src, dst, target, send_sem, recv_sem):
        here = jnp.logical_and(target[0] == me_i, target[1] == me_j)

        @pl.when(here)
        def _():
            pltpu.make_async_copy(src, dst, recv_sem).start()

        @pl.when(jnp.logical_not(here))
        def _():
            remote(src, dst, target, send_sem, recv_sem)

    def sent(src, target, send_sem):
        here = jnp.logical_and(target[0] == me_i, target[1] == me_j)

        @pl.when(jnp.logical_not(here))
        def _():
            done(src, send_sem)

    def done(ref, sem):
        pltpu.make_async_copy(ref, ref, sem).wait()

    def partner(t):
        dy, dx, dc = lax.div(t, n_rcv), lax.div(lax.rem(t, n_rcv), 2), lax.rem(t, 2)
        py = lax.rem(y + dy, side)
        px = lax.rem(lax.div(me_j, 2) + dx, n_rcv // 2)
        pj = px * 2 + lax.rem(me_j + dc, 2)
        return py, pj

    def source(t):
        dy, dx, dc = lax.div(t, n_rcv), lax.div(lax.rem(t, n_rcv), 2), lax.rem(t, 2)
        py = lax.rem(y + side - dy, side)
        px = lax.rem(lax.div(me_j, 2) + n_rcv // 2 - dx, n_rcv // 2)
        pj = px * 2 + lax.rem(me_j + dc, 2)
        return py, pj

    def freq(s, py, pj):
        return s * plane + py * n_rcv + pj

    def d_block(s, i, j):
        return dbuf.at[s, j, :, rows_of(i, own_rows), :]

    def p_block(s, b, j):
        return pbuf.at[s, b, rows_of(j, own_pts), :]

    def send_d(s, t):
        py, pj = partner(t)
        remote(
            d_ref.at[:, freq(s, py, pj)], d_block(s, me_i, me_j), (plane_base + py, pj),
            d_send.at[s, t], d_recv.at[s, me_i, 0, me_j],
        )

    def send_p(s, t):
        py, pj = partner(t)
        remote(
            rec.at[freq(s, py, pj)], p_block(s, b_me, me_j), (plane_base + py, pj),
            p_send.at[s, t], p_recv.at[s, b_me, me_j],
        )

    def d_unit(s, i, q, j):
        return dbuf.at[s, j, :, rows_of(i * cuts + q, unit), :]

    def pass_on(src, dst, s, i, q, j, to_left, to_right):
        for way, there, target in ((0, to_left, left), (1, to_right, right)):
            @pl.when(there)
            def _():
                remote(src, dst, target, dl_send.at[way, s, i], d_recv.at[s, i, q, j])

    def my_f(s):
        return freq(s, y, me_j)

    def for_slots(start, stop, body):
        each(0, slots, lambda s: each(start, stop, lambda t: body(s, t)))

    def p_up(s, t):
        py, pj = source(t)
        b = half * side + py
        done(p_block(s, b, pj), p_recv.at[s, b, pj])
        remote(p_block(s, b, pj), p_block(s, b, pj), head, pl_send.at[s, b], p_recv.at[s, b, pj])

    def row_up(s, k):
        i = far_base + lax.rem(y + side - k, side)

        def arrival(t):
            pj = source(t)[1]
            done(d_block(s, i, pj), d_recv.at[s, i, 0, pj])

        each(jnp.where(k == 0, 1, 0), n_rcv, arrival)

        def one(n):
            q, pj = lax.div(n, n_rcv), source(lax.rem(n, n_rcv))[1]
            block = d_unit(s, i, q, pj)
            sems = dl_send.at[0, s, i], d_recv.at[s, i, q, pj]

            @pl.when(jnp.logical_and(k == 0, pj == me_j))
            def _():
                remote(d_ref.at[:, my_f(s), rows_of(q, unit), :], block, head, *sems)

            @pl.when(jnp.logical_not(jnp.logical_and(k == 0, pj == me_j)))
            def _():
                remote(block, block, head, *sems)

        each(0, cuts * n_rcv, one)

    def settle(s, t):
        done(d_ref.at[:, 0], d_send.at[s, t])
        done(rec.at[0], p_send.at[s, t])

    @pl.when(relay)
    def _():
        def own_p(s):
            remote(
                rec.at[my_f(s)], p_block(s, b_me, me_j), head, pl_send.at[s, b_me], p_recv.at[s, b_me, me_j]
            )

        each(0, slots, own_p)
        for_slots(1, plane, send_p)
        for_slots(1, plane, send_d)
        for_slots(1, plane, p_up)
        for_slots(0, side, row_up)
        for_slots(1, plane, settle)

    def forwards(other):
        from_left = other < group
        return jnp.logical_and(has_left, jnp.logical_not(from_left)), jnp.logical_and(has_right, from_left)

    def take_far(s, k, q, start, stop):
        i = far_base + lax.rem(y + side - k, side)

        def one(t):
            pj = source(t)[1]
            block = d_unit(s, i, q, pj)
            done(block, d_recv.at[s, i, q, pj])
            pass_on(block, block, s, i, q, pj, has_left, has_right)

        each(start, stop, one)
        return i * cuts + q

    def take_other_near(s, hh, k):
        other = lax.rem(group + hh, n_groups)
        i = other * near + owner_half(other) * side + lax.rem(y + side - k, side)

        def one(j):
            block = d_block(s, i, j)
            done(block, d_recv.at[s, i, 0, j])
            if n_groups > 2:
                pass_on(block, block, s, i, 0, j, *forwards(other))

        each(0, n_rcv, one)
        return i

    def take_other_far(s, hh, k, q):
        other = lax.rem(group + hh, n_groups)
        i = other * near + (1 - owner_half(other)) * side + lax.rem(y + side - k, side)

        def one(j):
            block = d_unit(s, i, q, j)
            done(block, d_recv.at[s, i, q, j])
            if n_groups > 2:
                pass_on(block, block, s, i, q, j, *forwards(other))

        each(0, n_rcv, one)
        return i * cuts + q

    def compute(s, i, size):
        rows = rows_of(i, size)
        per_rcv = own_pts // size
        j = lax.div(i, per_rcv)

        def one(n):
            b = lax.rem(n + b_me, near)
            total = None
            for h in range(n_rcv):
                block = pbuf[s, b, h * own_pts:(h + 1) * own_pts, :]
                lhs = dbuf[s, h, :, rows, :].reshape(2 * size, own_pts)
                prod = jnp.dot(lhs, block, preferred_element_type=jnp.float32)
                total = prod if total is None else total + prod
            m_re = total[:size, :own_shots] - total[size:, own_shots:]
            m_im = total[:size, own_shots:] + total[size:, :own_shots]
            mbuf[s, b, rows, :own_shots] = m_re.astype(jnp.bfloat16)
            mbuf[s, b, rows, own_shots:] = m_im.astype(jnp.bfloat16)
            p_re = pbuf[s, b, rows, :own_shots].astype(jnp.float32)
            p_im = pbuf[s, b, rows, own_shots:].astype(jnp.float32)

            def down(value):
                return jnp.sum(value.reshape(size // 8, 8, own_shots), axis=0)

            acc[s, b, 0] += down(m_re * p_re + m_im * p_im)
            acc[s, b, 1] += down(m_re * p_im - m_im * p_re)
            acc[s, b, 2] += down(m_re * m_re + m_im * m_im)

        for n in range(near):
            one(n)

        def give(n):
            b = lax.rem(n + b_me, near)
            dst = o_ref.at[my_f(s), rows_of(lax.rem(i, per_rcv), size), :]
            send(mbuf.at[s, b, rows, :], dst, (group * near + b, j), o_send.at[s, b, j], o_recv.at[my_f(s)])

        each(0, near, give)

    def coefficients(s):
        def one(n):
            b = lax.rem(n + b_me, near)
            num_re, num_im, power = (
                jnp.sum(acc[s, b, v], axis=0, keepdims=True) / float(points) for v in range(3)
            )
            power = power + 1e-6
            row = lax.broadcasted_iota(jnp.int32, (8, own_shots), 0)
            fbuf[s, b] = jnp.where(row < 4, num_re / power, num_im / power)
            for j in range(n_rcv):
                send(
                    fbuf.at[s, b], filt_ref.at[my_f(s)], (group * near + b, j),
                    f_send.at[s, b, j], f_recv.at[my_f(s)],
                )

        each(0, near, one)

    def results(s, n):
        b, j = lax.div(n, n_rcv), lax.rem(n, n_rcv)
        target = (group * near + b, j)
        sent(fbuf.at[s, b], target, f_send.at[s, b, j])
        sent(mbuf.at[s, b, rows_of(j, own_pts), :], target, o_send.at[s, b, j])

    @pl.when(owner)
    def _():
        def own_d(s):
            src = d_ref.at[:, my_f(s)]
            pass_on(src, d_block(s, me_i, me_j), s, me_i, 0, me_j, has_left, has_right)
            pltpu.make_async_copy(src, d_block(s, me_i, me_j), d_recv.at[s, me_i, 0, me_j]).start()
            pltpu.make_async_copy(
                rec.at[my_f(s)], p_block(s, b_me, me_j), p_recv.at[s, b_me, me_j]
            ).start()

        each(0, slots, own_d)
        for_slots(1, plane, send_d)
        for_slots(1, plane, send_p)

        def in_plane(s, t):
            py, pj = source(t)
            i = own_base + py
            block = d_block(s, i, pj)
            done(block, d_recv.at[s, i, 0, pj])
            pass_on(block, block, s, i, 0, pj, has_left, has_right)

        for_slots(1, plane, in_plane)

        def first_ready(s):
            done(d_block(s, me_i, me_j), d_recv.at[s, me_i, 0, me_j])
            each(0, n_near, lambda n: done(
                p_block(s, lax.div(n, n_rcv), lax.rem(n, n_rcv)), p_recv.at[s, lax.div(n, n_rcv), lax.rem(n, n_rcv)]
            ))

        n_first = n_groups * side

        def first(n):
            s, r = lax.div(n, n_first), lax.rem(n, n_first)
            hh, k = lax.div(r, side), lax.rem(r, side)

            @pl.when(r == 0)
            def _():
                first_ready(s)

            @pl.when(hh > 0)
            def _():
                take_other_near(s, hh, k)

            other = lax.rem(group + hh, n_groups)
            compute(s, other * near + owner_half(other) * side + lax.rem(y + side - k, side), own_rows)

        each(0, n_first, first)
        for_slots(1, plane, settle)

        def place_of(u):
            s, r = lax.div(u, side * cuts), lax.rem(u, side * cuts)
            return s, lax.div(r, cuts), lax.rem(r, cuts)

        def others(u):
            s, k, q = place_of(u)
            each(1, n_groups, lambda hh: compute(s, take_other_far(s, hh, k, q), unit))
            pl.when(lax.rem(u, side * cuts) == side * cuts - 1)(lambda: coefficients(s))

        n_units = slots * side * cuts
        share = (slots - 1) * n_first // (n_units // 2)

        def second(u):
            s, k, q = place_of(u)
            early = n_rcv // 2

            @pl.when(u < n_units)
            def _():
                take_far(s, k, q, 0, early)

            @pl.when(u > 0)
            def _():
                others(u - 1)

            @pl.when(u < n_units)
            def _():
                compute(s, take_far(s, k, q, early, n_rcv), unit)

            @pl.when(jnp.logical_and(u > 0, u <= n_units // 2))
            def _():
                each(n_first + (u - 1) * share, n_first + u * share, first)

        each(0, n_units + 1, second)
        for_slots(0, n_near, lambda s, n: pl.when(s < slots - 1)(lambda: results(s, n)))

    def rows_sent(way, s, i):
        done(dbuf.at[s, :, :, rows_of(i, own_rows), :], dl_send.at[way, s, i])

    @pl.when(relay)
    def _():
        def one(s, k):
            rows_sent(0, s, far_base + k)
            done(pbuf.at[s, half * side + k], pl_send.at[s, half * side + k])

        for_slots(0, side, one)

    @pl.when(owner)
    def _():
        first_row, end_row = group * near, group * near + near
        pl.when(has_left)(lambda: for_slots(first_row, n_shot, lambda s, i: rows_sent(0, s, i)))
        pl.when(has_right)(lambda: for_slots(0, end_row, lambda s, i: rows_sent(1, s, i)))

    def result_arrived(n):
        done(o_ref.at[n], o_recv.at[n])
        done(filt_ref.at[n], f_recv.at[n])

    each(0, n_freq, result_arrived)

    @pl.when(owner)
    def _():
        each(0, n_near, lambda n: results(slots - 1, n))


def subtract_kernel(step, o_ref, filt_ref, rec_ref, pred_ref, prim_ref, pred_v, prim_v, out_sem):
    n_freq, shots = o_ref.shape[0], o_ref.shape[2] // 2

    def one(f):
        re, im = o_ref[f, :, :shots], o_ref[f, :, shots:]
        pred_v[0, f] = re
        pred_v[1, f] = im
        re, im = re.astype(jnp.float32), im.astype(jnp.float32)
        filt_re, filt_im = filt_ref[f, 0:1, :], filt_ref[f, 4:5, :]
        rec_re = rec_ref[f, :, :shots].astype(jnp.float32)
        rec_im = rec_ref[f, :, shots:].astype(jnp.float32)
        prim_v[0, f] = (rec_re - (filt_re * re - filt_im * im)).astype(jnp.bfloat16)
        prim_v[1, f] = (rec_im - (filt_re * im + filt_im * re)).astype(jnp.bfloat16)

    def copies(c):
        part = pl.ds(c * step, step)
        return [
            pltpu.make_async_copy(src.at[:, part], dst.at[:, part], out_sem.at[n, c])
            for n, (src, dst) in enumerate(((pred_v, pred_ref), (prim_v, prim_ref)))
        ]

    for c in range(n_freq // step):
        for n in range(step):
            one(c * step + n)
        for copy in copies(c):
            copy.start()
    for c in range(n_freq // step):
        for copy in copies(c):
            copy.wait()


def shards(n_shot, n_rcv, data_matrix, shot_records, live):
    _, n_freq, own_rows, own_pts = data_matrix.shape
    own_shots = shot_records.shape[3]
    points = own_pts * n_rcv
    side, cuts = 2, 2
    slots, near = n_freq // (side * n_rcv), 2 * side
    anywhere = pl.BlockSpec(memory_space=pl.ANY)
    dma = pltpu.SemaphoreType.DMA
    held = pltpu.VMEM((n_freq, own_pts, 2 * own_shots), jnp.bfloat16)
    multiples, filt, records = pl.pallas_call(
        functools.partial(exchange_kernel, n_shot, n_rcv, side, cuts),
        out_shape=(held, pltpu.VMEM((n_freq, 8, own_shots), jnp.float32), held),
        in_specs=[pl.BlockSpec(memory_space=pltpu.HBM)] * 3,
        out_specs=(anywhere, anywhere, pl.BlockSpec(memory_space=pltpu.VMEM)),
        scratch_shapes=[
            pltpu.VMEM((slots, n_rcv, 2, points, own_pts), jnp.bfloat16),
            pltpu.VMEM((slots, near, points, 2 * own_shots), jnp.bfloat16),
            pltpu.VMEM((2, n_freq, own_pts, own_shots), jnp.bfloat16),
            pltpu.VMEM((own_pts, own_shots), jnp.int32),
            pltpu.VMEM((slots, near, points, 2 * own_shots), jnp.bfloat16),
            pltpu.VMEM((slots, near, 8, own_shots), jnp.float32),
            pltpu.VMEM((slots, near, 3, 8, own_shots), jnp.float32),
            dma((2,)),
            dma((slots, side * n_rcv)),
            dma((slots, n_shot, cuts, n_rcv)),
            dma((2, slots, n_shot)),
            dma((slots, side * n_rcv)),
            dma((slots, near, n_rcv)),
            dma((slots, near)),
            dma((slots, near, n_rcv)),
            dma((n_freq,)),
            dma((slots, near, n_rcv)),
            dma((n_freq,)),
        ],
        compiler_params=pltpu.CompilerParams(
            collective_id=0, has_side_effects=True, vmem_limit_bytes=61280 * 1024
        ),
    )(data_matrix, shot_records, live)
    step = 2
    out = jax.ShapeDtypeStruct((2, n_freq, own_pts, own_shots), jnp.bfloat16)
    whole = pl.BlockSpec(memory_space=pltpu.VMEM)
    return pl.pallas_call(
        functools.partial(subtract_kernel, step),
        out_shape=(out, out),
        in_specs=[whole] * 3,
        out_specs=(anywhere, anywhere),
        scratch_shapes=[
            pltpu.VMEM((2, n_freq, own_pts, own_shots), jnp.bfloat16),
            pltpu.VMEM((2, n_freq, own_pts, own_shots), jnp.bfloat16),
            dma((2, n_freq // step)),
        ],
        compiler_params=pltpu.CompilerParams(vmem_limit_bytes=24 * 1024 * 1024),
    )(multiples, filt, records)


def solution(mesh):
    in_specs = (P(None, None, "shot", "rcv"), P(None, None, "rcv", "shot"), P("rcv", "shot"))
    out_specs = (P(None, None, "rcv", "shot"), P(None, None, "rcv", "shot"))
    body = functools.partial(shards, mesh.shape["shot"], mesh.shape["rcv"])
    return jax.shard_map(body, mesh=mesh, in_specs=in_specs, out_specs=out_specs, check_vma=False)
```

```python
import functools

import jax
import jax.numpy as jnp
from jax import lax
from jax.experimental import pallas as pl
from jax.experimental.pallas import tpu as pltpu
from jax.sharding import PartitionSpec as P

MESH = pl.DeviceIdType.MESH


def each(start, stop, body):
    def step(index, carry):
        body(index)
        return carry

    lax.fori_loop(start, stop, step, 0)


def exchange_kernel(
    n_shot, n_rcv, side, cuts,
    d_ref, s_ref, live_ref, o_ref, filt_ref, rec,
    dbuf, pbuf, srec, live_v, mbuf, fbuf, acc,
    load_sem, d_send, d_recv, dl_send, p_send, p_recv, pl_send, o_send, o_recv, f_send, f_recv,
):
    n_freq, own_rows = d_ref.shape[1], d_ref.shape[2]
    own_pts, own_shots = s_ref.shape[2], s_ref.shape[3]
    points = own_pts * n_rcv
    plane = side * n_rcv
    slots = n_freq // plane
    near = 2 * side
    n_groups = n_shot // near
    unit = own_rows // cuts
    me_i, me_j = lax.axis_index("shot"), lax.axis_index("rcv")
    group, b_me = lax.div(me_i, near), lax.rem(me_i, near)
    half, y = lax.div(b_me, side), lax.rem(me_i, side)
    place = y * n_rcv + me_j

    def owner_half(g):
        return jnp.where(g < n_groups // 2, 1, 0)

    mine = owner_half(group)
    owner = half == mine
    relay = jnp.logical_not(owner)
    own_base = group * near + mine * side
    far_base = group * near + (1 - mine) * side
    plane_base = group * near + half * side
    has_left = jnp.logical_and(owner, group > 0)
    has_right = jnp.logical_and(owner, group < n_groups - 1)
    left = ((group - 1) * near + owner_half(group - 1) * side + y, me_j)
    right = ((group + 1) * near + owner_half(group + 1) * side + y, me_j)
    head = (own_base + y, me_j)

    load_s = pltpu.make_async_copy(s_ref, srec, load_sem.at[0])
    load_live = pltpu.make_async_copy(live_ref, live_v, load_sem.at[1])
    load_s.start()
    load_live.start()

    barrier = pltpu.get_barrier_semaphore()
    n_near = near * n_rcv

    def greet(k):
        other = lax.rem(place + k, plane)
        target = (plane_base + lax.div(other, n_rcv), lax.rem(other, n_rcv))
        pl.semaphore_signal(barrier, inc=1, device_id=target, device_id_type=MESH)

    facing = (group * near + (1 - half) * side + y, me_j)
    pl.semaphore_signal(barrier, inc=1, device_id=facing, device_id_type=MESH)
    for there, target in ((has_left, left), (has_right, right)):
        @pl.when(there)
        def _():
            pl.semaphore_signal(barrier, inc=1, device_id=target, device_id_type=MESH)

    each(1, plane, greet)
    def mask(f):
        keep = live_v[...].astype(jnp.bfloat16)
        rec[f, :, :own_shots] = srec[0, f] * keep
        rec[f, :, own_shots:] = srec[1, f] * keep

    def mask_records():
        load_s.wait()
        load_live.wait()
        each(0, n_freq, mask)

    pl.when(relay)(mask_records)
    acc[...] = jnp.zeros_like(acc)
    pl.semaphore_wait(barrier, plane + has_left.astype(jnp.int32) + has_right.astype(jnp.int32))

    def rows_of(i, size):
        return pl.ds(pl.multiple_of(i * size, size), size)

    def remote(src, dst, target, send_sem, recv_sem):
        pltpu.make_async_remote_copy(
            src_ref=src, dst_ref=dst, send_sem=send_sem, recv_sem=recv_sem,
            device_id=target, device_id_type=MESH,
        ).start()

    def send(src, dst, target, send_sem, recv_sem):
        here = jnp.logical_and(target[0] == me_i, target[1] == me_j)

        @pl.when(here)
        def _():
            pltpu.make_async_copy(src, dst, recv_sem).start()

        @pl.when(jnp.logical_not(here))
        def _():
            remote(src, dst, target, send_sem, recv_sem)

    def sent(src, target, send_sem):
        here = jnp.logical_and(target[0] == me_i, target[1] == me_j)

        @pl.when(jnp.logical_not(here))
        def _():
            done(src, send_sem)

    def done(ref, sem):
        pltpu.make_async_copy(ref, ref, sem).wait()

    def partner(t):
        dy, dx, dc = lax.div(t, n_rcv), lax.div(lax.rem(t, n_rcv), 2), lax.rem(t, 2)
        py = lax.rem(y + dy, side)
        px = lax.rem(lax.div(me_j, 2) + dx, n_rcv // 2)
        pj = px * 2 + lax.rem(me_j + dc, 2)
        return py, pj

    def source(t):
        dy, dx, dc = lax.div(t, n_rcv), lax.div(lax.rem(t, n_rcv), 2), lax.rem(t, 2)
        py = lax.rem(y + side - dy, side)
        px = lax.rem(lax.div(me_j, 2) + n_rcv // 2 - dx, n_rcv // 2)
        pj = px * 2 + lax.rem(me_j + dc, 2)
        return py, pj

    def freq(s, py, pj):
        return s * plane + py * n_rcv + pj

    def d_block(s, i, j):
        return dbuf.at[s, j, :, rows_of(i, own_rows), :]

    def p_block(s, b, j):
        return pbuf.at[s, b, rows_of(j, own_pts), :]

    def send_d(s, t):
        py, pj = partner(t)
        remote(
            d_ref.at[:, freq(s, py, pj)], d_block(s, me_i, me_j), (plane_base + py, pj),
            d_send.at[s, t], d_recv.at[s, me_i, 0, me_j],
        )

    def send_p(s, t):
        py, pj = partner(t)
        remote(
            rec.at[freq(s, py, pj)], p_block(s, b_me, me_j), (plane_base + py, pj),
            p_send.at[s, t], p_recv.at[s, b_me, me_j],
        )

    def d_unit(s, i, q, j):
        return dbuf.at[s, j, :, rows_of(i * cuts + q, unit), :]

    def split(s):
        return jnp.logical_and(s == 0, lax.rem(me_j, 2) == 0)

    def pass_on(src, dst, s, i, q, j, *ways):
        for way, (there, target) in enumerate(zip(ways, (facing, left, right))):
            if there is not None:
                @pl.when(there)
                def _():
                    remote(src, dst, target, dl_send.at[way, s, i], d_recv.at[s, i, q, j])

    def my_f(s):
        return freq(s, y, me_j)

    def for_slots(start, stop, body):
        each(0, slots, lambda s: each(start, stop, lambda t: body(s, t)))

    def p_up(s, t):
        py, pj = source(t)
        b = half * side + py

        @pl.when(jnp.logical_not(split(s)))
        def _():
            done(p_block(s, b, pj), p_recv.at[s, b, pj])
            remote(p_block(s, b, pj), p_block(s, b, pj), head, pl_send.at[s, b], p_recv.at[s, b, pj])

    def row_up(s, k):
        i = far_base + lax.rem(y + side - k, side)

        def arrival(t):
            pj = source(t)[1]
            done(d_block(s, i, pj), d_recv.at[s, i, 0, pj])

        each(jnp.where(k == 0, 1, 0), n_rcv, arrival)

        def one(n):
            q, t = lax.div(n, n_rcv), lax.rem(n, n_rcv)
            pj = source(t)[1]
            block = d_unit(s, i, q, pj)

            @pl.when(k + t > 0)
            def _():
                remote(block, block, head, dl_send.at[0, s, i], d_recv.at[s, i, q, pj])

            @pl.when(jnp.logical_and(k + t == 0, jnp.logical_not(split(s))))
            def _():
                own_unit(s, q)

        each(0, cuts * n_rcv, one)

    def own_unit(s, q):
        remote(
            d_ref.at[:, my_f(s), rows_of(q, unit), :], d_unit(s, me_i, q, me_j), head,
            dl_send.at[0, s, me_i], d_recv.at[s, me_i, q, me_j],
        )

    def keep_d(s):
        pltpu.make_async_copy(
            d_ref.at[:, my_f(s)], d_block(s, me_i, me_j), d_recv.at[s, me_i, 0, me_j]
        ).start()

    def keep_p(s):
        pltpu.make_async_copy(rec.at[my_f(s)], p_block(s, b_me, me_j), p_recv.at[s, b_me, me_j]).start()

    def settle(s, t):
        done(d_ref.at[:, 0], d_send.at[s, t])
        done(rec.at[0], p_send.at[s, t])

    @pl.when(relay)
    def _():
        def own_p(s):
            @pl.when(split(s))
            def _():
                keep_p(s)
                keep_d(s)
                each(0, cuts, lambda q: own_unit(s, q))

            @pl.when(jnp.logical_not(split(s)))
            def _():
                remote(
                    rec.at[my_f(s)], p_block(s, b_me, me_j), head, pl_send.at[s, b_me], p_recv.at[s, b_me, me_j]
                )

        each(0, slots, own_p)
        for_slots(1, plane, send_p)
        for_slots(1, plane, send_d)
        for_slots(1, plane, p_up)
        for_slots(0, side, row_up)
        for_slots(1, plane, settle)

    def forwards(other):
        from_left = other < group
        return jnp.logical_and(has_left, jnp.logical_not(from_left)), jnp.logical_and(has_right, from_left)

    def take_far(s, k, q, start, stop):
        i = far_base + lax.rem(y + side - k, side)

        def one(t):
            pj = source(t)[1]
            block = d_unit(s, i, q, pj)
            done(block, d_recv.at[s, i, q, pj])
            pass_on(block, block, s, i, q, pj, None, has_left, has_right)

        each(start, stop, one)
        return i * cuts + q

    def take_other(s, hh, k, q, near_plane):
        other = lax.rem(group + hh, n_groups)
        nearer = owner_half(other)
        i = other * near + (nearer if near_plane else 1 - nearer) * side + lax.rem(y + side - k, side)

        def one(j):
            block = d_block(s, i, j) if near_plane else d_unit(s, i, q, j)
            done(block, d_recv.at[s, i, q, j])
            down = jnp.logical_and(owner, split(s))
            pass_on(block, block, s, i, q, j, down, *(forwards(other) if n_groups > 2 else ()))

        each(0, n_rcv, one)
        return i if near_plane else i * cuts + q

    def compute(s, i, size, planes):
        first_b, n_b = ((1 - half) if planes == 2 else half) * side, planes * side
        rows = rows_of(i, size)
        per_rcv = own_pts // size
        j = lax.div(i, per_rcv)

        def one(n):
            b = lax.rem(n + first_b, near)
            total = None
            for h in range(n_rcv):
                block = pbuf[s, b, h * own_pts:(h + 1) * own_pts, :]
                lhs = dbuf[s, h, :, rows, :].reshape(2 * size, own_pts)
                prod = jnp.dot(lhs, block, preferred_element_type=jnp.float32)
                total = prod if total is None else total + prod
            m_re = total[:size, :own_shots] - total[size:, own_shots:]
            m_im = total[:size, own_shots:] + total[size:, :own_shots]
            mbuf[s, b, rows, :own_shots] = m_re.astype(jnp.bfloat16)
            mbuf[s, b, rows, own_shots:] = m_im.astype(jnp.bfloat16)
            p_re = pbuf[s, b, rows, :own_shots].astype(jnp.float32)
            p_im = pbuf[s, b, rows, own_shots:].astype(jnp.float32)

            def down(value):
                return jnp.sum(value.reshape(size // 8, 8, own_shots), axis=0)

            acc[s, b, 0] += down(m_re * p_re + m_im * p_im)
            acc[s, b, 1] += down(m_re * p_im - m_im * p_re)
            acc[s, b, 2] += down(m_re * m_re + m_im * m_im)

        for n in range(n_b):
            one(n)

        def give(n):
            b = lax.rem(n + first_b, near)
            dst = o_ref.at[my_f(s), rows_of(lax.rem(i, per_rcv), size), :]
            send(mbuf.at[s, b, rows, :], dst, (group * near + b, j), o_send.at[s, b, j], o_recv.at[my_f(s)])

        each(0, n_b, give)

    def compute_owned(s, i, size):
        pl.when(split(s))(lambda: compute(s, i, size, 1))
        pl.when(jnp.logical_not(split(s)))(lambda: compute(s, i, size, 2))

    def shots_of(s):
        return jnp.where(split(s), half, 1 - half) * side, jnp.where(split(s), side, near)

    def coefficients(s):
        row = lax.broadcasted_iota(jnp.int32, (8, own_shots), 0)
        for b in range(near):
            num_re, num_im, power = (
                jnp.sum(acc[s, b, v], axis=0, keepdims=True) / float(points) for v in range(3)
            )
            power = power + 1e-6
            fbuf[s, b] = jnp.where(row < 4, num_re / power, num_im / power)
        first_b, n_b = shots_of(s)

        def give(n):
            b, j = lax.rem(lax.div(n, n_rcv) + first_b, near), lax.rem(n, n_rcv)
            send(
                fbuf.at[s, b], filt_ref.at[my_f(s)], (group * near + b, j),
                f_send.at[s, b, j], f_recv.at[my_f(s)],
            )

        each(0, n_b * n_rcv, give)

    def results_sent(s):
        first_b, n_b = shots_of(s)

        def one(n):
            b, j = lax.rem(lax.div(n, n_rcv) + first_b, near), lax.rem(n, n_rcv)
            target = (group * near + b, j)
            sent(fbuf.at[s, b], target, f_send.at[s, b, j])
            sent(mbuf.at[s, b, rows_of(j, own_pts), :], target, o_send.at[s, b, j])

        each(0, n_b * n_rcv, one)

    @pl.when(jnp.logical_and(relay, split(0)))
    def _():
        done(d_block(0, me_i, me_j), d_recv.at[0, me_i, 0, me_j])

        def arrival(t):
            py, pj = source(t)
            b = half * side + py
            done(p_block(0, b, pj), p_recv.at[0, b, pj])

        each(0, plane, arrival)
        each(0, side, lambda k: compute(0, plane_base + k, own_rows, 1))

        def owner_rows(k):
            i = own_base + lax.rem(y + side - k, side)
            each(0, n_rcv, lambda j: done(d_block(0, i, j), d_recv.at[0, i, 0, j]))
            compute(0, i, own_rows, 1)

        each(0, side, owner_rows)
        each(1, n_groups, lambda hh: each(
            0, side, lambda k: compute(0, take_other(0, hh, k, 0, True), own_rows, 1)
        ))
        each(0, side * cuts, lambda r: each(1, n_groups, lambda hh: compute(
            0, take_other(0, hh, lax.div(r, cuts), lax.rem(r, cuts), False), unit, 1
        )))
        coefficients(0)

    @pl.when(owner)
    def _():
        def own_d(s):
            src = d_ref.at[:, my_f(s)]
            pass_on(src, d_block(s, me_i, me_j), s, me_i, 0, me_j, split(s), has_left, has_right)
            keep_d(s)

        each(0, slots, own_d)
        for_slots(1, plane, send_d)
        mask_records()
        each(0, slots, keep_p)
        for_slots(1, plane, send_p)

        def in_plane(s, t):
            py, pj = source(t)
            i = own_base + py
            block = d_block(s, i, pj)
            done(block, d_recv.at[s, i, 0, pj])
            pass_on(block, block, s, i, 0, pj, split(s), has_left, has_right)

        for_slots(1, plane, in_plane)

        def first_ready(s):
            done(d_block(s, me_i, me_j), d_recv.at[s, me_i, 0, me_j])
            first_b, n_b = shots_of(s)

            def arrival(n):
                b, j = lax.rem(lax.div(n, n_rcv) + first_b, near), lax.rem(n, n_rcv)
                done(p_block(s, b, j), p_recv.at[s, b, j])

            each(0, n_b * n_rcv, arrival)

        n_first = n_groups * side

        def first(n):
            s, r = lax.div(n, n_first), lax.rem(n, n_first)
            hh, k = lax.div(r, side), lax.rem(r, side)

            @pl.when(r == 0)
            def _():
                first_ready(s)

            @pl.when(hh > 0)
            def _():
                take_other(s, hh, k, 0, True)

            other = lax.rem(group + hh, n_groups)
            compute_owned(s, other * near + owner_half(other) * side + lax.rem(y + side - k, side), own_rows)

        each(0, n_first, first)
        for_slots(1, plane, settle)

        def place_of(u):
            s, r = lax.div(u, side * cuts), lax.rem(u, side * cuts)
            return s, lax.div(r, cuts), lax.rem(r, cuts)

        def others(u):
            s, k, q = place_of(u)
            each(1, n_groups, lambda hh: compute_owned(s, take_other(s, hh, k, q, False), unit))
            pl.when(lax.rem(u, side * cuts) == side * cuts - 1)(lambda: coefficients(s))

        n_units = slots * side * cuts
        later = (slots - 1) * n_first
        spread = n_units // 2

        def second(u):
            s, k, q = place_of(u)

            @pl.when(u < n_units)
            def _():
                compute_owned(s, take_far(s, k, q, 0, n_rcv), unit)

            @pl.when(u > 0)
            def _():
                others(u - 1)

            @pl.when(jnp.logical_and(u > 0, u <= spread))
            def _():
                start, stop = (lax.div(n * later, spread) for n in (u - 1, u))
                each(n_first + start, n_first + stop, first)

        each(0, n_units + 1, second)

    def rows_sent(way, s, i):
        done(dbuf.at[s, :, :, rows_of(i, own_rows), :], dl_send.at[way, s, i])

    @pl.when(relay)
    def _():
        def one(s, k):
            rows_sent(0, s, plane_base + k)
            pl.when(jnp.logical_not(split(s)))(
                lambda: done(pbuf.at[s, half * side + k], pl_send.at[s, half * side + k])
            )

        for_slots(0, side, one)
        pl.when(split(0))(lambda: results_sent(0))

    @pl.when(owner)
    def _():
        first_row, end_row = group * near, group * near + near

        @pl.when(split(0))
        def _():
            each(0, side, lambda k: rows_sent(0, 0, own_base + k))
            each(0, first_row, lambda i: rows_sent(0, 0, i))
            each(end_row, n_shot, lambda i: rows_sent(0, 0, i))

        pl.when(has_left)(lambda: for_slots(first_row, n_shot, lambda s, i: rows_sent(1, s, i)))
        pl.when(has_right)(lambda: for_slots(0, end_row, lambda s, i: rows_sent(2, s, i)))
        each(0, slots, results_sent)

    def result_arrived(n):
        done(o_ref.at[n], o_recv.at[n])
        done(filt_ref.at[n], f_recv.at[n])

    each(0, n_freq, result_arrived)


def subtract_kernel(step, o_ref, filt_ref, rec_ref, pred_ref, prim_ref, pred_v, prim_v, out_sem):
    n_freq, shots = o_ref.shape[0], o_ref.shape[2] // 2

    def one(f):
        re, im = o_ref[f, :, :shots], o_ref[f, :, shots:]
        pred_v[0, f] = re
        pred_v[1, f] = im
        re, im = re.astype(jnp.float32), im.astype(jnp.float32)
        filt_re, filt_im = filt_ref[f, 0:1, :], filt_ref[f, 4:5, :]
        rec_re = rec_ref[f, :, :shots].astype(jnp.float32)
        rec_im = rec_ref[f, :, shots:].astype(jnp.float32)
        prim_v[0, f] = (rec_re - (filt_re * re - filt_im * im)).astype(jnp.bfloat16)
        prim_v[1, f] = (rec_im - (filt_re * im + filt_im * re)).astype(jnp.bfloat16)

    def copies(c):
        part = pl.ds(c * step, step)
        return [
            pltpu.make_async_copy(src.at[:, part], dst.at[:, part], out_sem.at[n, c])
            for n, (src, dst) in enumerate(((pred_v, pred_ref), (prim_v, prim_ref)))
        ]

    for c in range(n_freq // step):
        for n in range(step):
            one(c * step + n)
        for copy in copies(c):
            copy.start()
    for c in range(n_freq // step):
        for copy in copies(c):
            copy.wait()


def shards(n_shot, n_rcv, data_matrix, shot_records, live):
    _, n_freq, own_rows, own_pts = data_matrix.shape
    own_shots = shot_records.shape[3]
    points = own_pts * n_rcv
    side, cuts = 2, 2
    slots, near = n_freq // (side * n_rcv), 2 * side
    anywhere = pl.BlockSpec(memory_space=pl.ANY)
    dma = pltpu.SemaphoreType.DMA
    held = pltpu.VMEM((n_freq, own_pts, 2 * own_shots), jnp.bfloat16)
    multiples, filt, records = pl.pallas_call(
        functools.partial(exchange_kernel, n_shot, n_rcv, side, cuts),
        out_shape=(held, pltpu.VMEM((n_freq, 8, own_shots), jnp.float32), held),
        in_specs=[pl.BlockSpec(memory_space=pltpu.HBM)] * 3,
        out_specs=(anywhere, anywhere, pl.BlockSpec(memory_space=pltpu.VMEM)),
        scratch_shapes=[
            pltpu.VMEM((slots, n_rcv, 2, points, own_pts), jnp.bfloat16),
            pltpu.VMEM((slots, near, points, 2 * own_shots), jnp.bfloat16),
            pltpu.VMEM((2, n_freq, own_pts, own_shots), jnp.bfloat16),
            pltpu.VMEM((own_pts, own_shots), jnp.int32),
            pltpu.VMEM((slots, near, points, 2 * own_shots), jnp.bfloat16),
            pltpu.VMEM((slots, near, 8, own_shots), jnp.float32),
            pltpu.VMEM((slots, near, 3, 8, own_shots), jnp.float32),
            dma((2,)),
            dma((slots, side * n_rcv)),
            dma((slots, n_shot, cuts, n_rcv)),
            dma((3, slots, n_shot)),
            dma((slots, side * n_rcv)),
            dma((slots, near, n_rcv)),
            dma((slots, near)),
            dma((slots, near, n_rcv)),
            dma((n_freq,)),
            dma((slots, near, n_rcv)),
            dma((n_freq,)),
        ],
        compiler_params=pltpu.CompilerParams(
            collective_id=0, has_side_effects=True, vmem_limit_bytes=61280 * 1024
        ),
    )(data_matrix, shot_records, live)
    step = 2
    out = jax.ShapeDtypeStruct((2, n_freq, own_pts, own_shots), jnp.bfloat16)
    whole = pl.BlockSpec(memory_space=pltpu.VMEM)
    return pl.pallas_call(
        functools.partial(subtract_kernel, step),
        out_shape=(out, out),
        in_specs=[whole] * 3,
        out_specs=(anywhere, anywhere),
        scratch_shapes=[
            pltpu.VMEM((2, n_freq, own_pts, own_shots), jnp.bfloat16),
            pltpu.VMEM((2, n_freq, own_pts, own_shots), jnp.bfloat16),
            dma((2, n_freq // step)),
        ],
        compiler_params=pltpu.CompilerParams(vmem_limit_bytes=24 * 1024 * 1024),
    )(multiples, filt, records)


def solution(mesh):
    in_specs = (P(None, None, "shot", "rcv"), P(None, None, "rcv", "shot"), P("rcv", "shot"))
    out_specs = (P(None, None, "rcv", "shot"), P(None, None, "rcv", "shot"))
    body = functools.partial(shards, mesh.shape["shot"], mesh.shape["rcv"])
    return jax.shard_map(body, mesh=mesh, in_specs=in_specs, out_specs=out_specs, check_vma=False)
```

```python
import functools

import jax
import jax.numpy as jnp
from jax import lax
from jax.experimental import pallas as pl
from jax.experimental.pallas import tpu as pltpu
from jax.sharding import PartitionSpec as P

MESH = pl.DeviceIdType.MESH


def each(start, stop, body):
    def step(index, carry):
        body(index)
        return carry

    lax.fori_loop(start, stop, step, 0)


def exchange_kernel(
    n_shot, n_rcv, side, cuts,
    d_ref, s_ref, live_ref, o_ref, filt_ref, rec,
    dbuf, pbuf, srec, live_v, mbuf, fbuf, acc,
    load_sem, d_send, d_recv, dl_send, p_send, p_recv, pl_send, o_send, o_recv, f_send, f_recv,
):
    n_freq, own_rows = d_ref.shape[1], d_ref.shape[2]
    own_pts, own_shots = s_ref.shape[2], s_ref.shape[3]
    points = own_pts * n_rcv
    plane = side * n_rcv
    slots = n_freq // plane
    near = 2 * side
    n_groups = n_shot // near
    unit = own_rows // cuts
    me_i, me_j = lax.axis_index("shot"), lax.axis_index("rcv")
    group, b_me = lax.div(me_i, near), lax.rem(me_i, near)
    half, y = lax.div(b_me, side), lax.rem(me_i, side)
    place = y * n_rcv + me_j

    def owner_half(g):
        return jnp.where(g < n_groups // 2, 1, 0)

    mine = owner_half(group)
    owner = half == mine
    relay = jnp.logical_not(owner)
    own_base = group * near + mine * side
    far_base = group * near + (1 - mine) * side
    plane_base = group * near + half * side
    has_left = jnp.logical_and(owner, group > 0)
    has_right = jnp.logical_and(owner, group < n_groups - 1)
    left = ((group - 1) * near + owner_half(group - 1) * side + y, me_j)
    right = ((group + 1) * near + owner_half(group + 1) * side + y, me_j)
    head = (own_base + y, me_j)

    load_s = pltpu.make_async_copy(s_ref, srec, load_sem.at[0])
    load_live = pltpu.make_async_copy(live_ref, live_v, load_sem.at[1])
    load_s.start()
    load_live.start()

    barrier = pltpu.get_barrier_semaphore()
    n_near = near * n_rcv

    def greet(k):
        other = lax.rem(place + k, plane)
        target = (plane_base + lax.div(other, n_rcv), lax.rem(other, n_rcv))
        pl.semaphore_signal(barrier, inc=1, device_id=target, device_id_type=MESH)

    facing = (group * near + (1 - half) * side + y, me_j)
    pl.semaphore_signal(barrier, inc=1, device_id=facing, device_id_type=MESH)
    for there, target in ((has_left, left), (has_right, right)):
        @pl.when(there)
        def _():
            pl.semaphore_signal(barrier, inc=1, device_id=target, device_id_type=MESH)

    each(1, plane, greet)
    def mask(f):
        keep = live_v[...].astype(jnp.bfloat16)
        rec[f, :, :own_shots] = srec[0, f] * keep
        rec[f, :, own_shots:] = srec[1, f] * keep

    def mask_records():
        load_s.wait()
        load_live.wait()
        each(0, n_freq, mask)

    pl.when(relay)(mask_records)
    acc[...] = jnp.zeros_like(acc)
    pl.semaphore_wait(barrier, plane + has_left.astype(jnp.int32) + has_right.astype(jnp.int32))

    def rows_of(i, size):
        return pl.ds(pl.multiple_of(i * size, size), size)

    def remote(src, dst, target, send_sem, recv_sem):
        pltpu.make_async_remote_copy(
            src_ref=src, dst_ref=dst, send_sem=send_sem, recv_sem=recv_sem,
            device_id=target, device_id_type=MESH,
        ).start()

    def send(src, dst, target, send_sem, recv_sem):
        here = jnp.logical_and(target[0] == me_i, target[1] == me_j)

        @pl.when(here)
        def _():
            pltpu.make_async_copy(src, dst, recv_sem).start()

        @pl.when(jnp.logical_not(here))
        def _():
            remote(src, dst, target, send_sem, recv_sem)

    def done(ref, sem):
        pltpu.make_async_copy(ref, ref, sem).wait()

    def partner(t):
        dy, dx, dc = lax.div(t, n_rcv), lax.div(lax.rem(t, n_rcv), 2), lax.rem(t, 2)
        py = lax.rem(y + dy, side)
        px = lax.rem(lax.div(me_j, 2) + dx, n_rcv // 2)
        pj = px * 2 + lax.rem(me_j + dc, 2)
        return py, pj

    def source(t):
        dy, dx, dc = lax.div(t, n_rcv), lax.div(lax.rem(t, n_rcv), 2), lax.rem(t, 2)
        py = lax.rem(y + side - dy, side)
        px = lax.rem(lax.div(me_j, 2) + n_rcv // 2 - dx, n_rcv // 2)
        pj = px * 2 + lax.rem(me_j + dc, 2)
        return py, pj

    def freq(s, py, pj):
        return s * plane + py * n_rcv + pj

    def d_block(s, i, j):
        return dbuf.at[s, j, :, rows_of(i, own_rows), :]

    def p_block(s, b, j):
        return pbuf.at[s, b, rows_of(j, own_pts), :]

    def send_d(s, t):
        py, pj = partner(t)
        remote(
            d_ref.at[:, freq(s, py, pj)], d_block(s, me_i, me_j), (plane_base + py, pj),
            d_send, d_recv.at[s, me_i, 0, me_j],
        )

    def send_p(s, t):
        py, pj = partner(t)
        remote(
            rec.at[freq(s, py, pj)], p_block(s, b_me, me_j), (plane_base + py, pj),
            p_send, p_recv.at[s, b_me, me_j],
        )

    def d_unit(s, i, q, j):
        return dbuf.at[s, j, :, rows_of(i * cuts + q, unit), :]

    def split(s):
        return jnp.logical_and(s == 0, lax.rem(me_j, 2) == 0)

    def pass_on(src, dst, s, i, q, j, *ways):
        for way, (there, target) in enumerate(zip(ways, (facing, left, right))):
            if there is not None:
                @pl.when(there)
                def _():
                    remote(src, dst, target, dl_send.at[way, s, i], d_recv.at[s, i, q, j])

    def my_f(s):
        return freq(s, y, me_j)

    def for_slots(start, stop, body):
        each(0, slots, lambda s: each(start, stop, lambda t: body(s, t)))

    def p_up(s, t):
        py, pj = source(t)
        b = half * side + py

        @pl.when(jnp.logical_not(split(s)))
        def _():
            done(p_block(s, b, pj), p_recv.at[s, b, pj])
            remote(p_block(s, b, pj), p_block(s, b, pj), head, pl_send.at[s, b], p_recv.at[s, b, pj])

    def row_up(s, k):
        i = far_base + lax.rem(y + side - k, side)

        def arrival(t):
            pj = source(t)[1]
            done(d_block(s, i, pj), d_recv.at[s, i, 0, pj])

        each(jnp.where(k == 0, 1, 0), n_rcv, arrival)

        def one(n):
            q, t = lax.div(n, n_rcv), lax.rem(n, n_rcv)
            pj = source(t)[1]
            block = d_unit(s, i, q, pj)

            @pl.when(k + t > 0)
            def _():
                remote(block, block, head, dl_send.at[0, s, i], d_recv.at[s, i, q, pj])

            @pl.when(jnp.logical_and(k + t == 0, jnp.logical_not(split(s))))
            def _():
                own_unit(s, q)

        each(0, cuts * n_rcv, one)

    def own_unit(s, q):
        remote(
            d_ref.at[:, my_f(s), rows_of(q, unit), :], d_unit(s, me_i, q, me_j), head,
            dl_send.at[0, s, me_i], d_recv.at[s, me_i, q, me_j],
        )

    def keep_d(s):
        pltpu.make_async_copy(
            d_ref.at[:, my_f(s)], d_block(s, me_i, me_j), d_recv.at[s, me_i, 0, me_j]
        ).start()

    def keep_p(s):
        pltpu.make_async_copy(rec.at[my_f(s)], p_block(s, b_me, me_j), p_recv.at[s, b_me, me_j]).start()

    def settle():
        done(d_ref.at[:, :slots * (plane - 1)], d_send)
        done(rec.at[:slots * (plane - 1)], p_send)

    @pl.when(relay)
    def _():
        def own_p(s):
            @pl.when(split(s))
            def _():
                keep_p(s)
                keep_d(s)
                each(0, cuts, lambda q: own_unit(s, q))

            @pl.when(jnp.logical_not(split(s)))
            def _():
                remote(
                    rec.at[my_f(s)], p_block(s, b_me, me_j), head, pl_send.at[s, b_me], p_recv.at[s, b_me, me_j]
                )

        each(0, slots, own_p)
        for_slots(1, plane, send_p)
        for_slots(1, plane, send_d)
        for_slots(1, plane, p_up)
        for_slots(0, side, row_up)
        settle()

    def forwards(other):
        from_left = other < group
        return jnp.logical_and(has_left, jnp.logical_not(from_left)), jnp.logical_and(has_right, from_left)

    def take_far(s, k, q, start, stop):
        i = far_base + lax.rem(y + side - k, side)

        def one(t):
            pj = source(t)[1]
            block = d_unit(s, i, q, pj)
            done(block, d_recv.at[s, i, q, pj])
            pass_on(block, block, s, i, q, pj, None, has_left, has_right)

        each(start, stop, one)
        return i * cuts + q

    def take_other(s, hh, k, q, near_plane):
        other = lax.rem(group + hh, n_groups)
        nearer = owner_half(other)
        i = other * near + (nearer if near_plane else 1 - nearer) * side + lax.rem(y + side - k, side)

        def one(j):
            block = d_block(s, i, j) if near_plane else d_unit(s, i, q, j)
            done(block, d_recv.at[s, i, q, j])
            down = jnp.logical_and(owner, split(s))
            pass_on(block, block, s, i, q, j, down, *(forwards(other) if n_groups > 2 else ()))

        each(0, n_rcv, one)
        return i if near_plane else i * cuts + q

    def compute(s, i, size, planes, last=False):
        first_b, n_b = ((1 - half) if planes == 2 else half) * side, planes * side
        rows = rows_of(i, size)
        per_rcv = own_pts // size
        j = lax.div(i, per_rcv)

        def one(n):
            b = lax.rem(n + first_b, near)
            total = None
            for h in range(n_rcv):
                block = pbuf[s, b, h * own_pts:(h + 1) * own_pts, :]
                lhs = dbuf[s, h, :, rows, :].reshape(2 * size, own_pts)
                prod = jnp.dot(lhs, block, preferred_element_type=jnp.float32)
                total = prod if total is None else total + prod
            m_re = total[:size, :own_shots] - total[size:, own_shots:]
            m_im = total[:size, own_shots:] + total[size:, :own_shots]
            mbuf[s, b, rows, :own_shots] = m_re.astype(jnp.bfloat16)
            mbuf[s, b, rows, own_shots:] = m_im.astype(jnp.bfloat16)
            p_re = pbuf[s, b, rows, :own_shots].astype(jnp.float32)
            p_im = pbuf[s, b, rows, own_shots:].astype(jnp.float32)

            def down(value):
                return jnp.sum(value.reshape(size // 8, 8, own_shots), axis=0)

            acc[s, b, 0] += down(m_re * p_re + m_im * p_im)
            acc[s, b, 1] += down(m_re * p_im - m_im * p_re)
            acc[s, b, 2] += down(m_re * m_re + m_im * m_im)

        for n in range(n_b):
            one(n)

        def give(n):
            b = lax.rem(n + first_b, near)
            dst = o_ref.at[my_f(s), rows_of(lax.rem(i, per_rcv), size), :]
            send(mbuf.at[s, b, rows, :], dst, (group * near + b, j), o_send.at[s], o_recv)

        if last is False:
            each(0, n_b, give)
        else:
            pl.when(last)(lambda: coefficients(s))
            each(0, n_b, give)

    def compute_owned(s, i, size, last=False):
        pl.when(split(s))(lambda: compute(s, i, size, 1, last))
        pl.when(jnp.logical_not(split(s)))(lambda: compute(s, i, size, 2, last))

    def shots_of(s):
        return jnp.where(split(s), half, 1 - half) * side, jnp.where(split(s), side, near)

    def coefficients(s):
        row = lax.broadcasted_iota(jnp.int32, (8, own_shots), 0)
        for b in range(near):
            num_re, num_im, power = (
                jnp.sum(acc[s, b, v], axis=0, keepdims=True) / float(points) for v in range(3)
            )
            power = power + 1e-6
            fbuf[s, b] = jnp.where(row < 4, num_re / power, num_im / power)
        first_b, n_b = shots_of(s)

        def give(n):
            b, j = lax.rem(lax.div(n, n_rcv) + first_b, near), lax.rem(n, n_rcv)
            send(
                fbuf.at[s, b], filt_ref.at[my_f(s)], (group * near + b, j),
                f_send.at[s], f_recv,
            )

        each(0, n_b * n_rcv, give)

    def results_sent(s):
        for some, n_b in ((split(s), side), (jnp.logical_not(split(s)), near)):
            @pl.when(some)
            def _():
                done(o_ref.at[:n_b * n_rcv - 1], o_send.at[s])
                done(filt_ref.at[:n_b * n_rcv - 1], f_send.at[s])

    @pl.when(jnp.logical_and(relay, split(0)))
    def _():
        done(d_block(0, me_i, me_j), d_recv.at[0, me_i, 0, me_j])

        def arrival(t):
            py, pj = source(t)
            b = half * side + py
            done(p_block(0, b, pj), p_recv.at[0, b, pj])

        each(0, plane, arrival)
        each(0, side, lambda k: compute(0, plane_base + k, own_rows, 1))

        def owner_rows(k):
            i = own_base + lax.rem(y + side - k, side)
            each(0, n_rcv, lambda j: done(d_block(0, i, j), d_recv.at[0, i, 0, j]))
            compute(0, i, own_rows, 1)

        each(0, side, owner_rows)
        each(1, n_groups, lambda hh: each(
            0, side, lambda k: compute(0, take_other(0, hh, k, 0, True), own_rows, 1)
        ))
        each(0, side * cuts, lambda r: each(1, n_groups, lambda hh: compute(
            0, take_other(0, hh, lax.div(r, cuts), lax.rem(r, cuts), False), unit, 1
        )))
        coefficients(0)

    @pl.when(owner)
    def _():
        def own_d(s):
            src = d_ref.at[:, my_f(s)]
            pass_on(src, d_block(s, me_i, me_j), s, me_i, 0, me_j, split(s), has_left, has_right)
            keep_d(s)

        each(0, slots, own_d)
        for_slots(1, plane, send_d)
        mask_records()
        each(0, slots, keep_p)
        for_slots(1, plane, send_p)

        def in_plane(s, t):
            py, pj = source(t)
            i = own_base + py
            block = d_block(s, i, pj)
            done(block, d_recv.at[s, i, 0, pj])
            pass_on(block, block, s, i, 0, pj, split(s), has_left, has_right)

        for_slots(1, plane, in_plane)

        def first_ready(s):
            done(d_block(s, me_i, me_j), d_recv.at[s, me_i, 0, me_j])
            first_b, n_b = shots_of(s)

            def arrival(n):
                b, j = lax.rem(lax.div(n, n_rcv) + first_b, near), lax.rem(n, n_rcv)
                done(p_block(s, b, j), p_recv.at[s, b, j])

            each(0, n_b * n_rcv, arrival)

        n_first = n_groups * side

        def first(n):
            s, r = lax.div(n, n_first), lax.rem(n, n_first)
            hh, k = lax.div(r, side), lax.rem(r, side)

            @pl.when(r == 0)
            def _():
                first_ready(s)

            @pl.when(hh > 0)
            def _():
                take_other(s, hh, k, 0, True)

            other = lax.rem(group + hh, n_groups)
            compute_owned(s, other * near + owner_half(other) * side + lax.rem(y + side - k, side), own_rows)

        each(0, n_first, first)
        settle()

        def place_of(u):
            s, r = lax.div(u, side * cuts), lax.rem(u, side * cuts)
            return s, lax.div(r, cuts), lax.rem(r, cuts)

        def others(u):
            s, k, q = place_of(u)
            end = lax.rem(u, side * cuts) == side * cuts - 1
            each(1, n_groups, lambda hh: compute_owned(
                s, take_other(s, hh, k, q, False), unit, jnp.logical_and(end, hh == n_groups - 1)
            ))

        n_units = slots * side * cuts
        later = (slots - 1) * n_first
        spread = n_units // 2

        def second(u):
            s, k, q = place_of(u)

            @pl.when(u < n_units)
            def _():
                compute_owned(s, take_far(s, k, q, 0, n_rcv), unit)

            @pl.when(u > 0)
            def _():
                others(u - 1)

            @pl.when(jnp.logical_and(u > 0, u <= spread))
            def _():
                start, stop = (lax.div(n * later, spread) for n in (u - 1, u))
                each(n_first + start, n_first + stop, first)

        each(0, n_units + 1, second)

    def rows_sent(way, s, i):
        done(dbuf.at[s, :, :, rows_of(i, own_rows), :], dl_send.at[way, s, i])

    @pl.when(relay)
    def _():
        def one(s, k):
            rows_sent(0, s, plane_base + k)
            pl.when(jnp.logical_not(split(s)))(
                lambda: done(pbuf.at[s, half * side + k], pl_send.at[s, half * side + k])
            )

        for_slots(0, side, one)
        pl.when(split(0))(lambda: results_sent(0))

    @pl.when(owner)
    def _():
        first_row, end_row = group * near, group * near + near

        @pl.when(split(0))
        def _():
            each(0, side, lambda k: rows_sent(0, 0, own_base + k))
            each(0, first_row, lambda i: rows_sent(0, 0, i))
            each(end_row, n_shot, lambda i: rows_sent(0, 0, i))

        pl.when(has_left)(lambda: for_slots(first_row, n_shot, lambda s, i: rows_sent(1, s, i)))
        pl.when(has_right)(lambda: for_slots(0, end_row, lambda s, i: rows_sent(2, s, i)))
        each(0, slots, results_sent)

    done(o_ref, o_recv)
    done(filt_ref, f_recv)


def subtract_kernel(step, o_ref, filt_ref, rec_ref, pred_ref, prim_ref, pred_v, prim_v, out_sem):
    n_freq, shots = o_ref.shape[0], o_ref.shape[2] // 2

    def one(f):
        re, im = o_ref[f, :, :shots], o_ref[f, :, shots:]
        pred_v[0, f] = re
        pred_v[1, f] = im
        re, im = re.astype(jnp.float32), im.astype(jnp.float32)
        filt_re, filt_im = filt_ref[f, 0:1, :], filt_ref[f, 4:5, :]
        rec_re = rec_ref[f, :, :shots].astype(jnp.float32)
        rec_im = rec_ref[f, :, shots:].astype(jnp.float32)
        prim_v[0, f] = (rec_re - (filt_re * re - filt_im * im)).astype(jnp.bfloat16)
        prim_v[1, f] = (rec_im - (filt_re * im + filt_im * re)).astype(jnp.bfloat16)

    def copies(c):
        part = pl.ds(c * step, step)
        return [
            pltpu.make_async_copy(src.at[:, part], dst.at[:, part], out_sem.at[n, c])
            for n, (src, dst) in enumerate(((pred_v, pred_ref), (prim_v, prim_ref)))
        ]

    for c in range(n_freq // step):
        for n in range(step):
            one(c * step + n)
        for copy in copies(c):
            copy.start()
    for c in range(n_freq // step):
        for copy in copies(c):
            copy.wait()


def shards(n_shot, n_rcv, data_matrix, shot_records, live):
    _, n_freq, own_rows, own_pts = data_matrix.shape
    own_shots = shot_records.shape[3]
    points = own_pts * n_rcv
    side, cuts = 2, 2
    slots, near = n_freq // (side * n_rcv), 2 * side
    anywhere = pl.BlockSpec(memory_space=pl.ANY)
    dma = pltpu.SemaphoreType.DMA
    held = pltpu.VMEM((n_freq, own_pts, 2 * own_shots), jnp.bfloat16)
    multiples, filt, records = pl.pallas_call(
        functools.partial(exchange_kernel, n_shot, n_rcv, side, cuts),
        out_shape=(held, pltpu.VMEM((n_freq, 8, own_shots), jnp.float32), held),
        in_specs=[pl.BlockSpec(memory_space=pltpu.HBM)] * 3,
        out_specs=(anywhere, anywhere, pl.BlockSpec(memory_space=pltpu.VMEM)),
        scratch_shapes=[
            pltpu.VMEM((slots, n_rcv, 2, points, own_pts), jnp.bfloat16),
            pltpu.VMEM((slots, near, points, 2 * own_shots), jnp.bfloat16),
            pltpu.VMEM((2, n_freq, own_pts, own_shots), jnp.bfloat16),
            pltpu.VMEM((own_pts, own_shots), jnp.int32),
            pltpu.VMEM((slots, near, points, 2 * own_shots), jnp.bfloat16),
            pltpu.VMEM((slots, near, 8, own_shots), jnp.float32),
            pltpu.VMEM((slots, near, 3, 8, own_shots), jnp.float32),
            dma((2,)),
            dma,
            dma((slots, n_shot, cuts, n_rcv)),
            dma((3, slots, n_shot)),
            dma,
            dma((slots, near, n_rcv)),
            dma((slots, near)),
            dma((slots,)),
            dma,
            dma((slots,)),
            dma,
        ],
        compiler_params=pltpu.CompilerParams(
            collective_id=0, has_side_effects=True, vmem_limit_bytes=61280 * 1024
        ),
    )(data_matrix, shot_records, live)
    step = 2
    out = jax.ShapeDtypeStruct((2, n_freq, own_pts, own_shots), jnp.bfloat16)
    whole = pl.BlockSpec(memory_space=pltpu.VMEM)
    return pl.pallas_call(
        functools.partial(subtract_kernel, step),
        out_shape=(out, out),
        in_specs=[whole] * 3,
        out_specs=(anywhere, anywhere),
        scratch_shapes=[
            pltpu.VMEM((2, n_freq, own_pts, own_shots), jnp.bfloat16),
            pltpu.VMEM((2, n_freq, own_pts, own_shots), jnp.bfloat16),
            dma((2, n_freq // step)),
        ],
        compiler_params=pltpu.CompilerParams(vmem_limit_bytes=24 * 1024 * 1024),
    )(multiples, filt, records)


def solution(mesh):
    in_specs = (P(None, None, "shot", "rcv"), P(None, None, "rcv", "shot"), P("rcv", "shot"))
    out_specs = (P(None, None, "rcv", "shot"), P(None, None, "rcv", "shot"))
    body = functools.partial(shards, mesh.shape["shot"], mesh.shape["rcv"])
    return jax.shard_map(body, mesh=mesh, in_specs=in_specs, out_specs=out_specs, check_vma=False)
```

```python
import functools

import jax
import jax.numpy as jnp
from jax import lax
from jax.experimental import pallas as pl
from jax.experimental.pallas import tpu as pltpu
from jax.sharding import PartitionSpec as P

MESH = pl.DeviceIdType.MESH


def each(start, stop, body):
    def step(index, carry):
        body(index)
        return carry

    lax.fori_loop(start, stop, step, 0)


def exchange_kernel(
    n_shot, n_rcv, side, cuts,
    d_ref, s_ref, live_ref, o_ref, filt_ref, rec,
    dbuf, pbuf, srec, live_v, mbuf, fbuf, acc,
    load_sem, d_send, d_recv, dl_send, p_send, p_recv, pl_send, o_send, o_recv, f_send, f_recv,
):
    n_freq, own_rows = d_ref.shape[1], d_ref.shape[2]
    own_pts, own_shots = s_ref.shape[2], s_ref.shape[3]
    points = own_pts * n_rcv
    plane = side * n_rcv
    slots = n_freq // plane
    near = 2 * side
    n_groups = n_shot // near
    unit = own_rows // cuts
    me_i, me_j = lax.axis_index("shot"), lax.axis_index("rcv")
    group, b_me = lax.div(me_i, near), lax.rem(me_i, near)
    half, y = lax.div(b_me, side), lax.rem(me_i, side)
    place = y * n_rcv + me_j

    def owner_half(g):
        return jnp.where(g < n_groups // 2, 1, 0)

    mine = owner_half(group)
    owner = half == mine
    relay = jnp.logical_not(owner)
    own_base = group * near + mine * side
    far_base = group * near + (1 - mine) * side
    plane_base = group * near + half * side
    has_left = jnp.logical_and(owner, group > 0)
    has_right = jnp.logical_and(owner, group < n_groups - 1)
    left = ((group - 1) * near + owner_half(group - 1) * side + y, me_j)
    right = ((group + 1) * near + owner_half(group + 1) * side + y, me_j)
    head = (own_base + y, me_j)

    load_s = pltpu.make_async_copy(s_ref, srec, load_sem.at[0])
    load_live = pltpu.make_async_copy(live_ref, live_v, load_sem.at[1])
    load_s.start()
    load_live.start()

    barrier = pltpu.get_barrier_semaphore()
    n_near = near * n_rcv

    def greet(k):
        other = lax.rem(place + k, plane)
        target = (plane_base + lax.div(other, n_rcv), lax.rem(other, n_rcv))
        pl.semaphore_signal(barrier, inc=1, device_id=target, device_id_type=MESH)

    facing = (group * near + (1 - half) * side + y, me_j)
    pl.semaphore_signal(barrier, inc=1, device_id=facing, device_id_type=MESH)
    for there, target in ((has_left, left), (has_right, right)):
        @pl.when(there)
        def _():
            pl.semaphore_signal(barrier, inc=1, device_id=target, device_id_type=MESH)

    each(1, plane, greet)
    def mask(f):
        keep = live_v[...].astype(jnp.bfloat16)
        rec[f, :, :own_shots] = srec[0, f] * keep
        rec[f, :, own_shots:] = srec[1, f] * keep

    def mask_records():
        load_s.wait()
        load_live.wait()
        each(0, n_freq, mask)

    pl.when(relay)(mask_records)
    acc[...] = jnp.zeros_like(acc)
    pl.semaphore_wait(barrier, plane + has_left.astype(jnp.int32) + has_right.astype(jnp.int32))

    def rows_of(i, size):
        return pl.ds(pl.multiple_of(i * size, size), size)

    def remote(src, dst, target, send_sem, recv_sem):
        pltpu.make_async_remote_copy(
            src_ref=src, dst_ref=dst, send_sem=send_sem, recv_sem=recv_sem,
            device_id=target, device_id_type=MESH,
        ).start()

    def send(src, dst, target, send_sem, recv_sem):
        here = jnp.logical_and(target[0] == me_i, target[1] == me_j)

        @pl.when(here)
        def _():
            pltpu.make_async_copy(src, dst, recv_sem).start()

        @pl.when(jnp.logical_not(here))
        def _():
            remote(src, dst, target, send_sem, recv_sem)

    def done(ref, sem):
        pltpu.make_async_copy(ref, ref, sem).wait()

    def partner(t):
        dy, dx, dc = lax.div(t, n_rcv), lax.div(lax.rem(t, n_rcv), 2), lax.rem(t, 2)
        py = lax.rem(y + dy, side)
        px = lax.rem(lax.div(me_j, 2) + dx, n_rcv // 2)
        pj = px * 2 + lax.rem(me_j + dc, 2)
        return py, pj

    def source(t):
        dy, dx, dc = lax.div(t, n_rcv), lax.div(lax.rem(t, n_rcv), 2), lax.rem(t, 2)
        py = lax.rem(y + side - dy, side)
        px = lax.rem(lax.div(me_j, 2) + n_rcv // 2 - dx, n_rcv // 2)
        pj = px * 2 + lax.rem(me_j + dc, 2)
        return py, pj

    def freq(s, py, pj):
        return s * plane + py * n_rcv + pj

    def d_block(s, i, j):
        return dbuf.at[s, j, :, rows_of(i, own_rows), :]

    def p_block(s, b, j):
        return pbuf.at[s, b, rows_of(j, own_pts), :]

    def send_d(s, t):
        py, pj = partner(t)
        remote(
            d_ref.at[:, freq(s, py, pj)], d_block(s, me_i, me_j), (plane_base + py, pj),
            d_send, d_recv.at[s, me_i, 0, me_j],
        )

    def send_p(s, t):
        py, pj = partner(t)
        remote(
            rec.at[freq(s, py, pj)], p_block(s, b_me, me_j), (plane_base + py, pj),
            p_send, p_recv.at[s, b_me, me_j],
        )

    def d_unit(s, i, q, j):
        return dbuf.at[s, j, :, rows_of(i * cuts + q, unit), :]

    def split(s):
        return jnp.logical_and(s == 0, lax.rem(me_j, 2) == 0)

    def pass_on(src, dst, s, i, q, j, *ways):
        for way, (there, target) in enumerate(zip(ways, (facing, left, right))):
            if there is not None:
                @pl.when(there)
                def _():
                    remote(src, dst, target, dl_send.at[way, s, i], d_recv.at[s, i, q, j])

    def my_f(s):
        return freq(s, y, me_j)

    def for_slots(start, stop, body):
        each(0, slots, lambda s: each(start, stop, lambda t: body(s, t)))

    def p_up(s, t):
        py, pj = source(t)
        b = half * side + py

        @pl.when(jnp.logical_not(split(s)))
        def _():
            done(p_block(s, b, pj), p_recv.at[s, b, pj])
            remote(p_block(s, b, pj), p_block(s, b, pj), head, pl_send.at[s, b], p_recv.at[s, b, pj])

    def row_up(s, k):
        i = far_base + lax.rem(y + side - k, side)

        def arrival(t):
            pj = source(t)[1]
            done(d_block(s, i, pj), d_recv.at[s, i, 0, pj])

        each(jnp.where(k == 0, 1, 0), n_rcv, arrival)

        def one(n):
            q, t = lax.div(n, n_rcv), lax.rem(n, n_rcv)
            pj = source(t)[1]
            block = d_unit(s, i, q, pj)

            @pl.when(k + t > 0)
            def _():
                remote(block, block, head, dl_send.at[0, s, i], d_recv.at[s, i, q, pj])

            @pl.when(jnp.logical_and(k + t == 0, jnp.logical_not(split(s))))
            def _():
                own_unit(s, q)

        each(0, cuts * n_rcv, one)

    def own_unit(s, q):
        remote(
            d_ref.at[:, my_f(s), rows_of(q, unit), :], d_unit(s, me_i, q, me_j), head,
            dl_send.at[0, s, me_i], d_recv.at[s, me_i, q, me_j],
        )

    def keep_d(s):
        pltpu.make_async_copy(
            d_ref.at[:, my_f(s)], d_block(s, me_i, me_j), d_recv.at[s, me_i, 0, me_j]
        ).start()

    def keep_p(s):
        pltpu.make_async_copy(rec.at[my_f(s)], p_block(s, b_me, me_j), p_recv.at[s, b_me, me_j]).start()

    def settle():
        done(d_ref.at[:, :slots * (plane - 1)], d_send)
        done(rec.at[:slots * (plane - 1)], p_send)

    @pl.when(relay)
    def _():
        def own_p(s):
            @pl.when(split(s))
            def _():
                keep_p(s)
                keep_d(s)
                each(0, cuts, lambda q: own_unit(s, q))

            @pl.when(jnp.logical_not(split(s)))
            def _():
                remote(
                    rec.at[my_f(s)], p_block(s, b_me, me_j), head, pl_send.at[s, b_me], p_recv.at[s, b_me, me_j]
                )

        each(0, slots, own_p)
        for_slots(1, plane, send_p)
        for_slots(1, plane, send_d)
        for_slots(1, plane, p_up)
        for_slots(0, side, row_up)
        settle()

    def forwards(other):
        from_left = other < group
        return jnp.logical_and(has_left, jnp.logical_not(from_left)), jnp.logical_and(has_right, from_left)

    def take_far(s, k, q, start, stop):
        i = far_base + lax.rem(y + side - k, side)

        def one(t):
            pj = source(t)[1]
            block = d_unit(s, i, q, pj)
            done(block, d_recv.at[s, i, q, pj])
            pass_on(block, block, s, i, q, pj, None, has_left, has_right)

        each(start, stop, one)
        return i * cuts + q

    def take_other(s, hh, k, q, near_plane):
        other = lax.rem(group + hh, n_groups)
        nearer = owner_half(other)
        i = other * near + (nearer if near_plane else 1 - nearer) * side + lax.rem(y + side - k, side)

        def one(j):
            block = d_block(s, i, j) if near_plane else d_unit(s, i, q, j)
            done(block, d_recv.at[s, i, q, j])
            down = jnp.logical_and(owner, split(s))
            pass_on(block, block, s, i, q, j, down, *(forwards(other) if n_groups > 2 else ()))

        each(0, n_rcv, one)
        return i if near_plane else i * cuts + q

    def compute(s, i, size, far, last=False):
        first_b = (1 - half if far else half) * side
        rows = rows_of(i, size)
        per_rcv = own_pts // size
        j = lax.div(i, per_rcv)

        def one(n):
            b = n + first_b
            total = None
            for h in range(n_rcv):
                block = pbuf[s, b, h * own_pts:(h + 1) * own_pts, :]
                lhs = dbuf[s, h, :, rows, :].reshape(2 * size, own_pts)
                prod = jnp.dot(lhs, block, preferred_element_type=jnp.float32)
                total = prod if total is None else total + prod
            m_re = total[:size, :own_shots] - total[size:, own_shots:]
            m_im = total[:size, own_shots:] + total[size:, :own_shots]
            mbuf[s, b, rows, :own_shots] = m_re.astype(jnp.bfloat16)
            mbuf[s, b, rows, own_shots:] = m_im.astype(jnp.bfloat16)
            p_re = pbuf[s, b, rows, :own_shots].astype(jnp.float32)
            p_im = pbuf[s, b, rows, own_shots:].astype(jnp.float32)

            def down(value):
                return jnp.sum(value.reshape(size // 8, 8, own_shots), axis=0)

            acc[s, b, 0] += down(m_re * p_re + m_im * p_im)
            acc[s, b, 1] += down(m_re * p_im - m_im * p_re)
            acc[s, b, 2] += down(m_re * m_re + m_im * m_im)

        for n in range(side):
            one(n)

        def give(n):
            b = n + first_b
            dst = o_ref.at[my_f(s), rows_of(lax.rem(i, per_rcv), size), :]
            send(mbuf.at[s, b, rows, :], dst, (group * near + b, j), o_send.at[s], o_recv)

        if last is not False:
            pl.when(last)(lambda: coefficients(s, first_b))
        each(0, side, give)

    def compute_owned(s, i, size, last=False):
        pl.when(jnp.logical_not(split(s)))(lambda: compute(s, i, size, True, last))
        compute(s, i, size, False, last)

    def shots_of(s):
        return jnp.where(split(s), half, 1 - half) * side, jnp.where(split(s), side, near)

    def coefficients(s, first_b):
        row = lax.broadcasted_iota(jnp.int32, (8, own_shots), 0)
        for n in range(side):
            b = n + first_b
            num_re, num_im, power = (
                jnp.sum(acc[s, b, v], axis=0, keepdims=True) / float(points) for v in range(3)
            )
            power = power + 1e-6
            fbuf[s, b] = jnp.where(row < 4, num_re / power, num_im / power)

        def give(n):
            b, j = lax.div(n, n_rcv) + first_b, lax.rem(n, n_rcv)
            send(fbuf.at[s, b], filt_ref.at[my_f(s)], (group * near + b, j), f_send.at[s], f_recv)

        each(0, plane, give)

    def results_sent(s):
        for some, n_b in ((split(s), side), (jnp.logical_not(split(s)), near)):
            @pl.when(some)
            def _():
                done(o_ref.at[:n_b * n_rcv - 1], o_send.at[s])
                done(filt_ref.at[:n_b * n_rcv - 1], f_send.at[s])

    @pl.when(jnp.logical_and(relay, split(0)))
    def _():
        done(d_block(0, me_i, me_j), d_recv.at[0, me_i, 0, me_j])

        def arrival(t):
            py, pj = source(t)
            b = half * side + py
            done(p_block(0, b, pj), p_recv.at[0, b, pj])

        each(0, plane, arrival)
        each(0, side, lambda k: compute(0, plane_base + k, own_rows, False))

        def owner_rows(k):
            i = own_base + lax.rem(y + side - k, side)
            each(0, n_rcv, lambda j: done(d_block(0, i, j), d_recv.at[0, i, 0, j]))
            compute(0, i, own_rows, False)

        each(0, side, owner_rows)
        each(1, n_groups, lambda hh: each(
            0, side, lambda k: compute(0, take_other(0, hh, k, 0, True), own_rows, False)
        ))
        each(0, side * cuts, lambda r: each(1, n_groups, lambda hh: compute(
            0, take_other(0, hh, lax.div(r, cuts), lax.rem(r, cuts), False), unit, False
        )))
        coefficients(0, half * side)

    @pl.when(owner)
    def _():
        def own_d(s):
            src = d_ref.at[:, my_f(s)]
            pass_on(src, d_block(s, me_i, me_j), s, me_i, 0, me_j, split(s), has_left, has_right)
            keep_d(s)

        each(0, slots, own_d)
        for_slots(1, plane, send_d)
        mask_records()
        each(0, slots, keep_p)
        for_slots(1, plane, send_p)

        def in_plane(s, t):
            py, pj = source(t)
            i = own_base + py
            block = d_block(s, i, pj)
            done(block, d_recv.at[s, i, 0, pj])
            pass_on(block, block, s, i, 0, pj, split(s), has_left, has_right)

        for_slots(1, plane, in_plane)

        def first_ready(s):
            done(d_block(s, me_i, me_j), d_recv.at[s, me_i, 0, me_j])
            first_b, n_b = shots_of(s)

            def arrival(n):
                b, j = lax.rem(lax.div(n, n_rcv) + first_b, near), lax.rem(n, n_rcv)
                done(p_block(s, b, j), p_recv.at[s, b, j])

            each(0, n_b * n_rcv, arrival)

        n_first = n_groups * side

        def first(n):
            s, r = lax.div(n, n_first), lax.rem(n, n_first)
            hh, k = lax.div(r, side), lax.rem(r, side)

            @pl.when(r == 0)
            def _():
                first_ready(s)

            @pl.when(hh > 0)
            def _():
                take_other(s, hh, k, 0, True)

            other = lax.rem(group + hh, n_groups)
            compute_owned(s, other * near + owner_half(other) * side + lax.rem(y + side - k, side), own_rows)

        each(0, n_first, first)
        settle()

        def place_of(u):
            s, r = lax.div(u, side * cuts), lax.rem(u, side * cuts)
            return s, lax.div(r, cuts), lax.rem(r, cuts)

        def others(u):
            s, k, q = place_of(u)
            end = lax.rem(u, side * cuts) == side * cuts - 1
            each(1, n_groups, lambda hh: compute_owned(
                s, take_other(s, hh, k, q, False), unit, jnp.logical_and(end, hh == n_groups - 1)
            ))

        n_units = slots * side * cuts
        later = (slots - 1) * n_first
        spread = n_units // 2

        def second(u):
            s, k, q = place_of(u)

            @pl.when(u < n_units)
            def _():
                compute_owned(s, take_far(s, k, q, 0, n_rcv), unit)

            @pl.when(u > 0)
            def _():
                others(u - 1)

            @pl.when(jnp.logical_and(u > 0, u <= spread))
            def _():
                start, stop = (lax.div(n * later, spread) for n in (u - 1, u))
                each(n_first + start, n_first + stop, first)

        each(0, n_units + 1, second)

    def rows_sent(way, s, i):
        done(dbuf.at[s, :, :, rows_of(i, own_rows), :], dl_send.at[way, s, i])

    @pl.when(relay)
    def _():
        def one(s, k):
            rows_sent(0, s, plane_base + k)
            pl.when(jnp.logical_not(split(s)))(
                lambda: done(pbuf.at[s, half * side + k], pl_send.at[s, half * side + k])
            )

        for_slots(0, side, one)
        pl.when(split(0))(lambda: results_sent(0))

    @pl.when(owner)
    def _():
        first_row, end_row = group * near, group * near + near

        @pl.when(split(0))
        def _():
            each(0, side, lambda k: rows_sent(0, 0, own_base + k))
            each(0, first_row, lambda i: rows_sent(0, 0, i))
            each(end_row, n_shot, lambda i: rows_sent(0, 0, i))

        pl.when(has_left)(lambda: for_slots(first_row, n_shot, lambda s, i: rows_sent(1, s, i)))
        pl.when(has_right)(lambda: for_slots(0, end_row, lambda s, i: rows_sent(2, s, i)))
        each(0, slots, results_sent)

    done(o_ref, o_recv)
    done(filt_ref, f_recv)


def subtract_kernel(step, o_ref, filt_ref, rec_ref, pred_ref, prim_ref, pred_v, prim_v, out_sem):
    n_freq, shots = o_ref.shape[0], o_ref.shape[2] // 2

    def one(f):
        re, im = o_ref[f, :, :shots], o_ref[f, :, shots:]
        pred_v[0, f] = re
        pred_v[1, f] = im
        re, im = re.astype(jnp.float32), im.astype(jnp.float32)
        filt_re, filt_im = filt_ref[f, 0:1, :], filt_ref[f, 4:5, :]
        rec_re = rec_ref[f, :, :shots].astype(jnp.float32)
        rec_im = rec_ref[f, :, shots:].astype(jnp.float32)
        prim_v[0, f] = (rec_re - (filt_re * re - filt_im * im)).astype(jnp.bfloat16)
        prim_v[1, f] = (rec_im - (filt_re * im + filt_im * re)).astype(jnp.bfloat16)

    def copies(c):
        part = pl.ds(c * step, step)
        return [
            pltpu.make_async_copy(src.at[:, part], dst.at[:, part], out_sem.at[n, c])
            for n, (src, dst) in enumerate(((pred_v, pred_ref), (prim_v, prim_ref)))
        ]

    for c in range(n_freq // step):
        for n in range(step):
            one(c * step + n)
        for copy in copies(c):
            copy.start()
    for c in range(n_freq // step):
        for copy in copies(c):
            copy.wait()


def shards(n_shot, n_rcv, data_matrix, shot_records, live):
    _, n_freq, own_rows, own_pts = data_matrix.shape
    own_shots = shot_records.shape[3]
    points = own_pts * n_rcv
    side, cuts = 2, 2
    slots, near = n_freq // (side * n_rcv), 2 * side
    anywhere = pl.BlockSpec(memory_space=pl.ANY)
    dma = pltpu.SemaphoreType.DMA
    held = pltpu.VMEM((n_freq, own_pts, 2 * own_shots), jnp.bfloat16)
    multiples, filt, records = pl.pallas_call(
        functools.partial(exchange_kernel, n_shot, n_rcv, side, cuts),
        out_shape=(held, pltpu.VMEM((n_freq, 8, own_shots), jnp.float32), held),
        in_specs=[pl.BlockSpec(memory_space=pltpu.HBM)] * 3,
        out_specs=(anywhere, anywhere, pl.BlockSpec(memory_space=pltpu.VMEM)),
        scratch_shapes=[
            pltpu.VMEM((slots, n_rcv, 2, points, own_pts), jnp.bfloat16),
            pltpu.VMEM((slots, near, points, 2 * own_shots), jnp.bfloat16),
            pltpu.VMEM((2, n_freq, own_pts, own_shots), jnp.bfloat16),
            pltpu.VMEM((own_pts, own_shots), jnp.int32),
            pltpu.VMEM((slots, near, points, 2 * own_shots), jnp.bfloat16),
            pltpu.VMEM((slots, near, 8, own_shots), jnp.float32),
            pltpu.VMEM((slots, near, 3, 8, own_shots), jnp.float32),
            dma((2,)),
            dma,
            dma((slots, n_shot, cuts, n_rcv)),
            dma((3, slots, n_shot)),
            dma,
            dma((slots, near, n_rcv)),
            dma((slots, near)),
            dma((slots,)),
            dma,
            dma((slots,)),
            dma,
        ],
        compiler_params=pltpu.CompilerParams(
            collective_id=0, has_side_effects=True, vmem_limit_bytes=61280 * 1024
        ),
    )(data_matrix, shot_records, live)
    step = 2
    out = jax.ShapeDtypeStruct((2, n_freq, own_pts, own_shots), jnp.bfloat16)
    whole = pl.BlockSpec(memory_space=pltpu.VMEM)
    return pl.pallas_call(
        functools.partial(subtract_kernel, step),
        out_shape=(out, out),
        in_specs=[whole] * 3,
        out_specs=(anywhere, anywhere),
        scratch_shapes=[
            pltpu.VMEM((2, n_freq, own_pts, own_shots), jnp.bfloat16),
            pltpu.VMEM((2, n_freq, own_pts, own_shots), jnp.bfloat16),
            dma((2, n_freq // step)),
        ],
        compiler_params=pltpu.CompilerParams(vmem_limit_bytes=24 * 1024 * 1024),
    )(multiples, filt, records)


def solution(mesh):
    in_specs = (P(None, None, "shot", "rcv"), P(None, None, "rcv", "shot"), P("rcv", "shot"))
    out_specs = (P(None, None, "rcv", "shot"), P(None, None, "rcv", "shot"))
    body = functools.partial(shards, mesh.shape["shot"], mesh.shape["rcv"])
    return jax.shard_map(body, mesh=mesh, in_specs=in_specs, out_specs=out_specs, check_vma=False)
```

```python
import functools

import jax
import jax.numpy as jnp
from jax import lax
from jax.experimental import pallas as pl
from jax.experimental.pallas import tpu as pltpu
from jax.sharding import PartitionSpec as P

MESH = pl.DeviceIdType.MESH


def each(start, stop, body):
    def step(index, carry):
        body(index)
        return carry

    lax.fori_loop(start, stop, step, 0)


def exchange_kernel(
    n_shot, n_rcv, side, cuts,
    d_ref, s_ref, live_ref, o_ref, filt_ref, rec,
    dbuf, pbuf, srec, live_v, mbuf, fbuf, acc,
    load_sem, d_send, d_recv, dl_send, p_send, p_recv, pl_send, o_send, o_recv, f_send, f_recv,
):
    n_freq, own_rows = d_ref.shape[1], d_ref.shape[2]
    own_pts, own_shots = s_ref.shape[2], s_ref.shape[3]
    points = own_pts * n_rcv
    plane = side * n_rcv
    slots = n_freq // plane
    near = 2 * side
    n_groups = n_shot // near
    unit = own_rows // cuts
    me_i, me_j = lax.axis_index("shot"), lax.axis_index("rcv")
    group, b_me = lax.div(me_i, near), lax.rem(me_i, near)
    half, y = lax.div(b_me, side), lax.rem(me_i, side)
    place = y * n_rcv + me_j

    def owner_half(g):
        return jnp.where(g < n_groups // 2, 1, 0)

    mine = owner_half(group)
    owner = half == mine
    relay = jnp.logical_not(owner)
    own_base = group * near + mine * side
    far_base = group * near + (1 - mine) * side
    plane_base = group * near + half * side
    has_left = jnp.logical_and(owner, group > 0)
    has_right = jnp.logical_and(owner, group < n_groups - 1)
    left = ((group - 1) * near + owner_half(group - 1) * side + y, me_j)
    right = ((group + 1) * near + owner_half(group + 1) * side + y, me_j)
    head = (own_base + y, me_j)

    load_s = pltpu.make_async_copy(s_ref, srec, load_sem.at[0])
    load_live = pltpu.make_async_copy(live_ref, live_v, load_sem.at[1])
    load_s.start()
    load_live.start()

    barrier = pltpu.get_barrier_semaphore()
    n_near = near * n_rcv

    def greet(k):
        other = lax.rem(place + k, plane)
        target = (plane_base + lax.div(other, n_rcv), lax.rem(other, n_rcv))
        pl.semaphore_signal(barrier, inc=1, device_id=target, device_id_type=MESH)

    facing = (group * near + (1 - half) * side + y, me_j)
    pl.semaphore_signal(barrier, inc=1, device_id=facing, device_id_type=MESH)
    for there, target in ((has_left, left), (has_right, right)):
        @pl.when(there)
        def _():
            pl.semaphore_signal(barrier, inc=1, device_id=target, device_id_type=MESH)

    each(1, plane, greet)
    def mask(f):
        keep = live_v[...].astype(jnp.bfloat16)
        rec[f, :, :own_shots] = srec[0, f] * keep
        rec[f, :, own_shots:] = srec[1, f] * keep

    def mask_records():
        load_s.wait()
        load_live.wait()
        each(0, n_freq, mask)

    pl.when(relay)(mask_records)
    acc[...] = jnp.zeros_like(acc)
    pl.semaphore_wait(barrier, plane + has_left.astype(jnp.int32) + has_right.astype(jnp.int32))

    def rows_of(i, size):
        return pl.ds(pl.multiple_of(i * size, size), size)

    def remote(src, dst, target, send_sem, recv_sem):
        pltpu.make_async_remote_copy(
            src_ref=src, dst_ref=dst, send_sem=send_sem, recv_sem=recv_sem,
            device_id=target, device_id_type=MESH,
        ).start()

    def send(src, dst, target, send_sem, recv_sem):
        here = jnp.logical_and(target[0] == me_i, target[1] == me_j)

        @pl.when(here)
        def _():
            pltpu.make_async_copy(src, dst, recv_sem).start()

        @pl.when(jnp.logical_not(here))
        def _():
            remote(src, dst, target, send_sem, recv_sem)

    def done(ref, sem):
        pltpu.make_async_copy(ref, ref, sem).wait()

    def partner(t):
        dy, dx, dc = lax.div(t, n_rcv), lax.div(lax.rem(t, n_rcv), 2), lax.rem(t, 2)
        py = lax.rem(y + dy, side)
        px = lax.rem(lax.div(me_j, 2) + dx, n_rcv // 2)
        pj = px * 2 + lax.rem(me_j + dc, 2)
        return py, pj

    def source(t):
        dy, dx, dc = lax.div(t, n_rcv), lax.div(lax.rem(t, n_rcv), 2), lax.rem(t, 2)
        py = lax.rem(y + side - dy, side)
        px = lax.rem(lax.div(me_j, 2) + n_rcv // 2 - dx, n_rcv // 2)
        pj = px * 2 + lax.rem(me_j + dc, 2)
        return py, pj

    def freq(s, py, pj):
        return s * plane + py * n_rcv + pj

    def d_block(s, i, j):
        return dbuf.at[s, j, :, rows_of(i, own_rows), :]

    def p_block(s, b, j):
        return pbuf.at[s, b, rows_of(j, own_pts), :]

    def send_d(s, t):
        py, pj = partner(t)
        remote(
            d_ref.at[:, freq(s, py, pj)], d_block(s, me_i, me_j), (plane_base + py, pj),
            d_send, d_recv.at[s, me_i, 0, me_j],
        )

    def send_p(s, t):
        py, pj = partner(t)
        remote(
            rec.at[freq(s, py, pj)], p_block(s, b_me, me_j), (plane_base + py, pj),
            p_send, p_recv.at[s, b_me, me_j],
        )

    def d_unit(s, i, q, j):
        return dbuf.at[s, j, :, rows_of(i * cuts + q, unit), :]

    def split(s):
        return jnp.logical_and(s == 0, lax.rem(me_j, 2) == 0)

    def pass_on(src, dst, s, i, q, j, *ways):
        for way, (there, target) in enumerate(zip(ways, (facing, left, right))):
            if there is not None:
                @pl.when(there)
                def _():
                    remote(src, dst, target, dl_send.at[way, s, i], d_recv.at[s, i, q, j])

    def my_f(s):
        return freq(s, y, me_j)

    def for_slots(start, stop, body):
        each(0, slots, lambda s: each(start, stop, lambda t: body(s, t)))

    def p_up(s, t):
        py, pj = source(t)
        b = half * side + py

        @pl.when(jnp.logical_not(split(s)))
        def _():
            done(p_block(s, b, pj), p_recv.at[s, b, pj])
            remote(p_block(s, b, pj), p_block(s, b, pj), head, pl_send.at[s, b], p_recv.at[s, b, pj])

    def row_up(s, k):
        i = far_base + lax.rem(y + side - k, side)

        def arrival(t):
            pj = source(t)[1]
            done(d_block(s, i, pj), d_recv.at[s, i, 0, pj])

        each(jnp.where(k == 0, 1, 0), n_rcv, arrival)

        def one(n):
            q, t = lax.div(n, n_rcv), lax.rem(n, n_rcv)
            pj = source(t)[1]
            block = d_unit(s, i, q, pj)

            @pl.when(k + t > 0)
            def _():
                remote(block, block, head, dl_send.at[0, s, i], d_recv.at[s, i, q, pj])

            @pl.when(jnp.logical_and(k + t == 0, jnp.logical_not(split(s))))
            def _():
                own_unit(s, q)

        each(0, cuts * n_rcv, one)

    def own_unit(s, q):
        remote(
            d_ref.at[:, my_f(s), rows_of(q, unit), :], d_unit(s, me_i, q, me_j), head,
            dl_send.at[0, s, me_i], d_recv.at[s, me_i, q, me_j],
        )

    def keep_d(s):
        pltpu.make_async_copy(
            d_ref.at[:, my_f(s)], d_block(s, me_i, me_j), d_recv.at[s, me_i, 0, me_j]
        ).start()

    def keep_p(s):
        pltpu.make_async_copy(rec.at[my_f(s)], p_block(s, b_me, me_j), p_recv.at[s, b_me, me_j]).start()

    def settle():
        done(d_ref.at[:, :slots * (plane - 1)], d_send)
        done(rec.at[:slots * (plane - 1)], p_send)

    @pl.when(relay)
    def _():
        def own_p(s):
            @pl.when(split(s))
            def _():
                keep_p(s)
                keep_d(s)
                each(0, cuts, lambda q: own_unit(s, q))

            @pl.when(jnp.logical_not(split(s)))
            def _():
                remote(
                    rec.at[my_f(s)], p_block(s, b_me, me_j), head, pl_send.at[s, b_me], p_recv.at[s, b_me, me_j]
                )

        each(0, slots, own_p)
        for_slots(1, plane, send_p)
        for_slots(1, plane, send_d)
        for_slots(1, plane, p_up)
        for_slots(0, side, row_up)
        settle()

    def forwards(other):
        from_left = other < group
        return jnp.logical_and(has_left, jnp.logical_not(from_left)), jnp.logical_and(has_right, from_left)

    def take_far(s, k, q, start, stop):
        i = far_base + lax.rem(y + side - k, side)

        def one(t):
            pj = source(t)[1]
            block = d_unit(s, i, q, pj)
            done(block, d_recv.at[s, i, q, pj])
            pass_on(block, block, s, i, q, pj, None, has_left, has_right)

        each(start, stop, one)
        return i * cuts + q

    def take_other(s, hh, k, q, near_plane):
        other = lax.rem(group + hh, n_groups)
        nearer = owner_half(other)
        i = other * near + (nearer if near_plane else 1 - nearer) * side + lax.rem(y + side - k, side)

        def one(j):
            block = d_block(s, i, j) if near_plane else d_unit(s, i, q, j)
            done(block, d_recv.at[s, i, q, j])
            down = jnp.logical_and(owner, split(s))
            pass_on(block, block, s, i, q, j, down, *(forwards(other) if n_groups > 2 else ()))

        each(0, n_rcv, one)
        return i if near_plane else i * cuts + q

    def compute(s, i, size, far, last=False):
        first_b = (1 - half if far else half) * side
        sems = o_send.at[s], o_recv
        rows = rows_of(i, size)
        per_rcv = own_pts // size
        j = lax.div(i, per_rcv)

        def one(n):
            b = n + first_b
            total = None
            for h in range(n_rcv):
                block = pbuf[s, b, h * own_pts:(h + 1) * own_pts, :]
                lhs = dbuf[s, h, :, rows, :].reshape(2 * size, own_pts)
                prod = jnp.dot(lhs, block, preferred_element_type=jnp.float32)
                total = prod if total is None else total + prod
            m_re = total[:size, :own_shots] - total[size:, own_shots:]
            m_im = total[:size, own_shots:] + total[size:, :own_shots]
            mbuf[s, b, rows, :own_shots] = m_re.astype(jnp.bfloat16)
            mbuf[s, b, rows, own_shots:] = m_im.astype(jnp.bfloat16)
            p_re = pbuf[s, b, rows, :own_shots].astype(jnp.float32)
            p_im = pbuf[s, b, rows, own_shots:].astype(jnp.float32)

            def down(value):
                return jnp.sum(value.reshape(size // 8, 8, own_shots), axis=0)

            acc[s, b, 0] += down(m_re * p_re + m_im * p_im)
            acc[s, b, 1] += down(m_re * p_im - m_im * p_re)
            acc[s, b, 2] += down(m_re * m_re + m_im * m_im)

        for n in range(side):
            one(n)

        def give(n):
            b = n + first_b
            dst = o_ref.at[my_f(s), rows_of(lax.rem(i, per_rcv), size), :]
            (remote if far else send)(mbuf.at[s, b, rows, :], dst, (group * near + b, j), *sems)

        if last is not False:
            pl.when(last)(lambda: coefficients(s, first_b, far))
        each(0, side, give)

    def compute_owned(s, i, size, last=False):
        pl.when(jnp.logical_not(split(s)))(lambda: compute(s, i, size, True, last))
        compute(s, i, size, False, last)

    def shots_of(s):
        return jnp.where(split(s), half, 1 - half) * side, jnp.where(split(s), side, near)

    def coefficients(s, first_b, far):
        row = lax.broadcasted_iota(jnp.int32, (8, own_shots), 0)
        for n in range(side):
            b = n + first_b
            num_re, num_im, power = (
                jnp.sum(acc[s, b, v], axis=0, keepdims=True) / float(points) for v in range(3)
            )
            power = power + 1e-6
            fbuf[s, b] = jnp.where(row < 4, num_re / power, num_im / power)

        def give(n):
            b, j = lax.div(n, n_rcv) + first_b, lax.rem(n, n_rcv)
            (remote if far else send)(
                fbuf.at[s, b], filt_ref.at[my_f(s)], (group * near + b, j), f_send.at[s], f_recv
            )

        each(0, plane, give)

    def results_sent(s):
        for some, n_b in ((split(s), side), (jnp.logical_not(split(s)), near)):
            @pl.when(some)
            def _():
                done(o_ref.at[:n_b * n_rcv - 1], o_send.at[s])
                done(filt_ref.at[:n_b * n_rcv - 1], f_send.at[s])

    @pl.when(jnp.logical_and(relay, split(0)))
    def _():
        done(d_block(0, me_i, me_j), d_recv.at[0, me_i, 0, me_j])

        def arrival(t):
            py, pj = source(t)
            b = half * side + py
            done(p_block(0, b, pj), p_recv.at[0, b, pj])

        each(0, plane, arrival)
        each(0, side, lambda k: compute(0, plane_base + k, own_rows, False))

        def owner_rows(k):
            i = own_base + lax.rem(y + side - k, side)
            each(0, n_rcv, lambda j: done(d_block(0, i, j), d_recv.at[0, i, 0, j]))
            compute(0, i, own_rows, False)

        each(0, side, owner_rows)
        each(1, n_groups, lambda hh: each(
            0, side, lambda k: compute(0, take_other(0, hh, k, 0, True), own_rows, False)
        ))
        each(0, side * cuts, lambda r: each(1, n_groups, lambda hh: compute(
            0, take_other(0, hh, lax.div(r, cuts), lax.rem(r, cuts), False), unit, False
        )))
        coefficients(0, half * side, False)

    @pl.when(owner)
    def _():
        def own_d(s):
            src = d_ref.at[:, my_f(s)]
            pass_on(src, d_block(s, me_i, me_j), s, me_i, 0, me_j, split(s), has_left, has_right)
            keep_d(s)

        each(0, slots, own_d)
        for_slots(1, plane, send_d)
        mask_records()
        each(0, slots, keep_p)
        for_slots(1, plane, send_p)

        def in_plane(s, t):
            py, pj = source(t)
            i = own_base + py
            block = d_block(s, i, pj)
            done(block, d_recv.at[s, i, 0, pj])
            pass_on(block, block, s, i, 0, pj, split(s), has_left, has_right)

        for_slots(1, plane, in_plane)

        def first_ready(s):
            done(d_block(s, me_i, me_j), d_recv.at[s, me_i, 0, me_j])
            first_b, n_b = shots_of(s)

            def arrival(n):
                b, j = lax.rem(lax.div(n, n_rcv) + first_b, near), lax.rem(n, n_rcv)
                done(p_block(s, b, j), p_recv.at[s, b, j])

            each(0, n_b * n_rcv, arrival)

        n_first = n_groups * side

        def first(n):
            s, r = lax.div(n, n_first), lax.rem(n, n_first)
            hh, k = lax.div(r, side), lax.rem(r, side)

            @pl.when(r == 0)
            def _():
                first_ready(s)

            @pl.when(hh > 0)
            def _():
                take_other(s, hh, k, 0, True)

            other = lax.rem(group + hh, n_groups)
            compute_owned(s, other * near + owner_half(other) * side + lax.rem(y + side - k, side), own_rows)

        each(0, n_first, first)
        settle()

        def place_of(u):
            s, r = lax.div(u, side * cuts), lax.rem(u, side * cuts)
            return s, lax.div(r, cuts), lax.rem(r, cuts)

        def others(u):
            s, k, q = place_of(u)
            end = lax.rem(u, side * cuts) == side * cuts - 1
            each(1, n_groups, lambda hh: compute_owned(
                s, take_other(s, hh, k, q, False), unit, jnp.logical_and(end, hh == n_groups - 1)
            ))

        n_units = slots * side * cuts
        later = (slots - 1) * n_first
        spread = n_units - 2

        def second(u):
            s, k, q = place_of(u)

            @pl.when(u < n_units)
            def _():
                compute_owned(s, take_far(s, k, q, 0, n_rcv), unit)

            @pl.when(u == n_units)
            def _():
                each(0, slots - 1, results_sent)

            @pl.when(u > 0)
            def _():
                others(u - 1)

            @pl.when(jnp.logical_and(u > 0, u <= spread))
            def _():
                start, stop = (lax.div(n * later, spread) for n in (u - 1, u))
                each(n_first + start, n_first + stop, first)

        each(0, n_units + 1, second)

    def rows_sent(way, s, i):
        done(dbuf.at[s, :, :, rows_of(i, own_rows), :], dl_send.at[way, s, i])

    @pl.when(relay)
    def _():
        def one(s, k):
            rows_sent(0, s, plane_base + k)
            pl.when(jnp.logical_not(split(s)))(
                lambda: done(pbuf.at[s, half * side + k], pl_send.at[s, half * side + k])
            )

        for_slots(0, side, one)
        pl.when(split(0))(lambda: results_sent(0))

    @pl.when(owner)
    def _():
        first_row, end_row = group * near, group * near + near

        @pl.when(split(0))
        def _():
            each(0, side, lambda k: rows_sent(0, 0, own_base + k))
            each(0, first_row, lambda i: rows_sent(0, 0, i))
            each(end_row, n_shot, lambda i: rows_sent(0, 0, i))

        pl.when(has_left)(lambda: for_slots(first_row, n_shot, lambda s, i: rows_sent(1, s, i)))
        pl.when(has_right)(lambda: for_slots(0, end_row, lambda s, i: rows_sent(2, s, i)))
        results_sent(slots - 1)

    done(o_ref, o_recv)
    done(filt_ref, f_recv)


def subtract_kernel(step, o_ref, filt_ref, rec_ref, pred_ref, prim_ref, pred_v, prim_v, out_sem):
    n_freq, shots = o_ref.shape[0], o_ref.shape[2] // 2

    def one(f):
        re, im = o_ref[f, :, :shots], o_ref[f, :, shots:]
        pred_v[0, f] = re
        pred_v[1, f] = im
        re, im = re.astype(jnp.float32), im.astype(jnp.float32)
        filt_re, filt_im = filt_ref[f, 0:1, :], filt_ref[f, 4:5, :]
        rec_re = rec_ref[f, :, :shots].astype(jnp.float32)
        rec_im = rec_ref[f, :, shots:].astype(jnp.float32)
        prim_v[0, f] = (rec_re - (filt_re * re - filt_im * im)).astype(jnp.bfloat16)
        prim_v[1, f] = (rec_im - (filt_re * im + filt_im * re)).astype(jnp.bfloat16)

    def copies(c):
        part = pl.ds(c * step, step)
        return [
            pltpu.make_async_copy(src.at[:, part], dst.at[:, part], out_sem.at[n, c])
            for n, (src, dst) in enumerate(((pred_v, pred_ref), (prim_v, prim_ref)))
        ]

    for c in range(n_freq // step):
        for n in range(step):
            one(c * step + n)
        for copy in copies(c):
            copy.start()
    for c in range(n_freq // step):
        for copy in copies(c):
            copy.wait()


def shards(n_shot, n_rcv, data_matrix, shot_records, live):
    _, n_freq, own_rows, own_pts = data_matrix.shape
    own_shots = shot_records.shape[3]
    points = own_pts * n_rcv
    side, cuts = 2, 2
    slots, near = n_freq // (side * n_rcv), 2 * side
    anywhere = pl.BlockSpec(memory_space=pl.ANY)
    dma = pltpu.SemaphoreType.DMA
    held = pltpu.VMEM((n_freq, own_pts, 2 * own_shots), jnp.bfloat16)
    multiples, filt, records = pl.pallas_call(
        functools.partial(exchange_kernel, n_shot, n_rcv, side, cuts),
        out_shape=(held, pltpu.VMEM((n_freq, 8, own_shots), jnp.float32), held),
        in_specs=[pl.BlockSpec(memory_space=pltpu.HBM)] * 3,
        out_specs=(anywhere, anywhere, pl.BlockSpec(memory_space=pltpu.VMEM)),
        scratch_shapes=[
            pltpu.VMEM((slots, n_rcv, 2, points, own_pts), jnp.bfloat16),
            pltpu.VMEM((slots, near, points, 2 * own_shots), jnp.bfloat16),
            pltpu.VMEM((2, n_freq, own_pts, own_shots), jnp.bfloat16),
            pltpu.VMEM((own_pts, own_shots), jnp.int32),
            pltpu.VMEM((slots, near, points, 2 * own_shots), jnp.bfloat16),
            pltpu.VMEM((slots, near, 8, own_shots), jnp.float32),
            pltpu.VMEM((slots, near, 3, 8, own_shots), jnp.float32),
            dma((2,)),
            dma,
            dma((slots, n_shot, cuts, n_rcv)),
            dma((3, slots, n_shot)),
            dma,
            dma((slots, near, n_rcv)),
            dma((slots, near)),
            dma((slots,)),
            dma,
            dma((slots,)),
            dma,
        ],
        compiler_params=pltpu.CompilerParams(
            collective_id=0, has_side_effects=True, vmem_limit_bytes=61280 * 1024
        ),
    )(data_matrix, shot_records, live)
    step = 2
    out = jax.ShapeDtypeStruct((2, n_freq, own_pts, own_shots), jnp.bfloat16)
    whole = pl.BlockSpec(memory_space=pltpu.VMEM)
    return pl.pallas_call(
        functools.partial(subtract_kernel, step),
        out_shape=(out, out),
        in_specs=[whole] * 3,
        out_specs=(anywhere, anywhere),
        scratch_shapes=[
            pltpu.VMEM((2, n_freq, own_pts, own_shots), jnp.bfloat16),
            pltpu.VMEM((2, n_freq, own_pts, own_shots), jnp.bfloat16),
            dma((2, n_freq // step)),
        ],
        compiler_params=pltpu.CompilerParams(vmem_limit_bytes=24 * 1024 * 1024),
    )(multiples, filt, records)


def solution(mesh):
    in_specs = (P(None, None, "shot", "rcv"), P(None, None, "rcv", "shot"), P("rcv", "shot"))
    out_specs = (P(None, None, "rcv", "shot"), P(None, None, "rcv", "shot"))
    body = functools.partial(shards, mesh.shape["shot"], mesh.shape["rcv"])
    return jax.shard_map(body, mesh=mesh, in_specs=in_specs, out_specs=out_specs, check_vma=False)
```
